512 devices in a mesh: dp: 16 (over x, y), expert: 32 (over z, core).
Axes of the slice: x: 4, y: 4, z: 16, core: 2. Of those that a mesh axis runs over, the one named last changes fastest.
Arguments:
- tokens: bfloat16 [8192, 1024], P(('dp', 'expert')), may hold values from -6 to 6
- upstream: bfloat16 [8192, 1024], P(('dp', 'expert')), may hold values from -6 to 6
- expert_ids: int32 [8192, 8], P(('dp', 'expert')), may hold values from 0 to 127, all different within a row; in each aligned block of 16 rows (0 to 15, 16 to 31, ...) at most 2 rows name the same one
- gates: float32 [8192, 8], P(('dp', 'expert')), may hold values from 0.05 to 1
- relocate: int32 [32, 4], replicated, may hold values from 0 to 1, as said below
- w_gate_up: bfloat16 [32, 16, 384, 1024], P('expert', 'dp'), may hold values from -0.1875 to 0.1875
- w_down: bfloat16 [32, 16, 192, 1024], P('expert', 'dp'), may hold values from -0.21875 to 0.21875
Outputs:
- grad_tokens: bfloat16 [8192, 1024], P(('dp', 'expert'))
- grad_gate_up: bfloat16 [32, 16, 384, 1024], P('expert', 'dp')
- grad_down: bfloat16 [32, 16, 192, 1024], P('expert', 'dp')
The draws below stay inside these ranges and needn't reach their ends.
Inputs may be any that keep to these rules, and one draw needn't show every extreme that they name: `expert_ids`: each row names 8 different experts; the rows of one device name one expert at most 2 times, and some device reaches 2. `relocate`: the first and the second half of the rows are equal; both values occur.
All inputs are finite; a program needn't handle non-finite values.
Results may differ from the reference program's by a relative error of at most 0.0064.
Values may be sent and summed in bfloat16 or wider, within the bound.
A program may use at most 64 MiB of HBM per device.

```python
import math
import jax
import jax.numpy as jnp
import numpy as np
from jax import lax

D = 1024
F = 768
SLICES = 4
TOP = 8
TOK_DEV = 16
FS = 192
SLOTS = 4
EXPERTS = 128
CAP = 2
TOKENS = 8192
N_DP = 16
N_EXPERT = 32


def draw_relocate(key, part):
    half_rows = N_EXPERT // 2
    entry_count = half_rows * SLOTS
    flat_bits = jax.random.randint(jax.random.fold_in(key, 11), (entry_count,), 0, 2, dtype=jnp.int32)
    order = jax.random.permutation(jax.random.fold_in(key, 23), entry_count).astype(jnp.int32)
    flat_bits = flat_bits.at[order[0]].set(0)
    flat_bits = flat_bits.at[order[1]].set(1)
    first_half = flat_bits.reshape(half_rows, SLOTS)
    return jnp.concatenate([first_half, first_half], axis=0)


def block_scale(stream_key, shape, cuts, smallest, high):
    gain, own = 1.0, jax.random.fold_in(stream_key, 6)
    for dim, shards_of in cuts:
        steps = jnp.exp(jax.random.uniform(jax.random.fold_in(own, dim), (shards_of,), jnp.float32, smallest / len(cuts), high / len(cuts)))
        gain = gain * jnp.repeat(steps, shape[dim] // shards_of).reshape([-1 if axis == dim else 1 for axis in range(len(shape))])
    return gain


def shared_out(key, own, number, rows, amount, top, reach, skew):
    sequence = jax.random.permutation(key, amount)
    packed, ordinary = shares(amount, rows * top, reach, skew, True), shares(amount, rows * top, reach, skew, False)
    places = jnp.arange(amount)

    def named(sizes, offset_by):
        used = int((sizes > 0).sum())
        fixed = max(1, used // 4)
        passed = fixed + (places - fixed + offset_by * (used - fixed)) % max(1, amount - fixed)
        return jnp.zeros((amount,), jnp.int32).at[sequence[jnp.where(places < fixed, places, passed)]].set(jnp.asarray(sizes, jnp.int32))

    sizes = jnp.where(number % 4 == 0, named(packed, number // 4), named(ordinary, number - number // 4 - 1))
    mixed = jax.random.permutation(jax.random.fold_in(own, 3), amount)
    donor, receiver = mixed[0:amount // 2 * 2:2], mixed[1:amount // 2 * 2:2]
    margin = jnp.minimum(sizes[donor] - 1, reach - sizes[receiver]) // 2
    margin = jnp.where((donor == sequence[0]) | (receiver == sequence[0]) | (sizes[receiver] == 0), 0, jnp.maximum(margin, 0))
    passed = jax.random.randint(jax.random.fold_in(own, 4), (amount // 2,), 0, 1 << 20) % (margin + 1)
    sizes = sizes.at[donor].add(-passed).at[receiver].add(passed)
    items = jnp.searchsorted(jnp.cumsum(sizes), jnp.arange(rows * top), side="right").astype(jnp.int32)
    grid = items.reshape(top, rows).T
    grid = grid[jax.random.permutation(jax.random.fold_in(own, 1), rows)]
    offset_by = jax.random.randint(jax.random.fold_in(own, 2), (rows, 1), 0, top)
    return jnp.take_along_axis(grid, (jnp.arange(top)[None, :] + offset_by) % top, axis=1)


def shares(amount, total, bound, lean, full):
    loads = [(1 << 20) // math.isqrt(rank ** lean) + 1 for rank in range(1, amount + 1)]
    largest = bound if full else min(bound, max(-(-total // amount), total * loads[0] // sum(loads)))
    least = 1 if total - largest >= amount - 1 else 0
    given, surplus = [largest] + [least] * (amount - 1), total - largest - least * (amount - 1)
    while surplus > 0:
        candidates = [i for i in range(1, amount) if given[i] < largest] or [i for i in range(1, amount) if given[i] < bound]
        whole, budget = sum([loads[i] for i in candidates]), surplus
        for i in candidates:
            extra = min(bound - given[i], max(1, budget * loads[i] // whole), surplus)
            given[i] = given[i] + extra
            surplus = surplus - extra
    return np.array(given)


def normal_values(stream_key, extent, spread, most, shards=(), held_as=jnp.bfloat16):
    array = spread * jax.random.normal(stream_key, extent, jnp.float32)
    if shards:
        array = array * block_scale(stream_key, extent, shards, -0.22, 0.18)
    return jnp.clip(array, -most, most).astype(held_as)


def setup_inputs(seed: int = 0) -> dict:
    seeds = jax.random.split(jax.random.key(seed), 8)
    tokens = normal_values(seeds[0], (TOKENS, D), 1.0, 6.0, ((0, 512),))
    upstream = normal_values(seeds[1], (TOKENS, D), 1.0, 6.0, ((0, 512),))
    expert_ids_keys = jax.random.split(jax.random.fold_in(seeds[2], 1), TOKENS // TOK_DEV)
    expert_ids_turns = jax.random.permutation(jax.random.fold_in(seeds[2], 3), TOKENS // TOK_DEV)
    expert_ids = jax.vmap(lambda own, number: shared_out(jax.random.fold_in(seeds[2], 2), own, number, TOK_DEV, EXPERTS, TOP, CAP, 2))(expert_ids_keys, expert_ids_turns).reshape((TOKENS, TOP))
    gates = jnp.clip(jnp.exp(math.log(1.0) - 2.9957323 * jax.random.uniform(seeds[3], (TOKENS, TOP), jnp.float32) ** block_scale(seeds[3], (TOKENS, TOP), ((0, 512),), -0.2, 0.2)), 0.05, 1.0)
    relocate = draw_relocate(jax.random.fold_in(seeds[7], 71), 0)
    w_gate_up = normal_values(seeds[5], (N_EXPERT, N_DP, 2 * FS, D), D ** -0.5, 0.1875, ((0, 32), (1, 16)))
    w_down = normal_values(seeds[6], (N_EXPERT, N_DP, FS, D), F ** -0.5, 0.21875, ((0, 32), (1, 16)))
    return dict(tokens=tokens, upstream=upstream, expert_ids=expert_ids, gates=gates, relocate=relocate, w_gate_up=w_gate_up, w_down=w_down)


def silu_parts(values_in):
    sigmoid_of = jax.nn.sigmoid(values_in)
    return values_in * sigmoid_of, sigmoid_of * (1.0 + values_in * (1.0 - sigmoid_of))


def reference(tokens, upstream, expert_ids, gates, relocate, w_gate_up, w_down):
    rows_most = N_DP * N_EXPERT * CAP
    pair_count = TOKENS * TOP
    flat_ids = expert_ids.reshape(pair_count)
    grouped = jnp.argsort(flat_ids, stable=True).astype(jnp.int32)
    expert_iota = jnp.arange(EXPERTS, dtype=jnp.int32)
    counts = jnp.sum((flat_ids[:, None] == expert_iota[None, :]).astype(jnp.int32), axis=0)
    offsets = (jnp.cumsum(counts) - counts).astype(jnp.int32)
    order_padded = jnp.concatenate([grouped, jnp.zeros((rows_most,), jnp.int32)])
    flat_gates = gates.reshape(pair_count)
    gate_up = w_gate_up.reshape(EXPERTS, SLICES, 2, FS, D)
    down_all = w_down.reshape(EXPERTS, SLICES, FS, D)
    contract_last = (((1,), (1,)), ((), ()))
    contract_first = (((0,), (0,)), ((), ()))

    def one_expert(dx_sum, expert):
        first_row = offsets[expert]
        picked = lax.dynamic_slice_in_dim(order_padded, first_row, rows_most)
        live_row = jnp.arange(rows_most, dtype=jnp.int32) < counts[expert]
        picked = jnp.where(live_row, picked, 0)
        token_row = picked // TOP
        x_rows = jnp.where(live_row[:, None], jnp.take(tokens, token_row, axis=0), jnp.zeros((), tokens.dtype))
        scaled = jnp.take(flat_gates, picked)[:, None] * jnp.take(upstream, token_row, axis=0).astype(jnp.float32)
        d_rows = jnp.where(live_row[:, None], scaled, 0.0).astype(jnp.bfloat16)
        pieces = gate_up[expert]
        gate_full = pieces[:, 0].reshape(F, D)
        up_full = pieces[:, 1].reshape(F, D)
        down_full = down_all[expert].reshape(F, D)
        gate_pre = lax.dot_general(x_rows, gate_full, contract_last, preferred_element_type=jnp.float32)
        up_pre = lax.dot_general(x_rows, up_full, contract_last, preferred_element_type=jnp.float32)
        activated, slope_of = silu_parts(gate_pre)
        hidden = (activated * up_pre).astype(jnp.bfloat16)
        hidden_grad = lax.dot_general(d_rows, down_full, contract_last, preferred_element_type=jnp.float32)
        gate_grad = (hidden_grad * up_pre * slope_of).astype(jnp.bfloat16)
        up_grad = (hidden_grad * activated).astype(jnp.bfloat16)
        grad_gate = lax.dot_general(gate_grad, x_rows, contract_first, preferred_element_type=jnp.float32)
        grad_up = lax.dot_general(up_grad, x_rows, contract_first, preferred_element_type=jnp.float32)
        grad_dn = lax.dot_general(hidden, d_rows, contract_first, preferred_element_type=jnp.float32)
        gate_sliced = gate_grad.reshape(rows_most, SLICES, FS).astype(jnp.float32)
        up_sliced = up_grad.reshape(rows_most, SLICES, FS).astype(jnp.float32)
        slice_part = jnp.einsum('rsf,sfd->rsd', gate_sliced, pieces[:, 0].astype(jnp.float32))
        slice_part = slice_part + jnp.einsum('rsf,sfd->rsd', up_sliced, pieces[:, 1].astype(jnp.float32))
        rounded = lax.optimization_barrier(slice_part.astype(jnp.bfloat16))
        dx_pair = jnp.sum(rounded.astype(jnp.float32), axis=1)
        dx_sum = dx_sum.at[token_row].add(jnp.where(live_row[:, None], dx_pair, 0.0))
        grad_pack = jnp.stack([grad_gate.reshape(SLICES, FS, D), grad_up.reshape(SLICES, FS, D)], axis=1)
        return dx_sum, (grad_pack.astype(jnp.bfloat16), grad_dn.reshape(SLICES, FS, D).astype(jnp.bfloat16))

    dx_sum, stacked = lax.scan(one_expert, jnp.zeros((TOKENS, D), jnp.float32), expert_iota)
    grads_gu, grads_dn = stacked
    col_iota = jnp.arange(N_EXPERT, dtype=jnp.int32)[:, None]
    partner = (col_iota + N_EXPERT // 2) % N_EXPERT
    own_col = jnp.broadcast_to(col_iota, (N_EXPERT, SLOTS))
    source = jnp.where(relocate == 1, partner, own_col)
    slot_iota = jnp.arange(SLOTS, dtype=jnp.int32)[None, :]
    moved_gu = grads_gu.reshape(N_EXPERT, SLOTS, SLICES, 2, FS, D)[source, slot_iota]
    moved_dn = grads_dn.reshape(N_EXPERT, SLOTS, SLICES, FS, D)[source, slot_iota]
    return (dx_sum.astype(jnp.bfloat16), moved_gu.reshape(N_EXPERT, N_DP, 2 * FS, D), moved_dn.reshape(N_EXPERT, N_DP, FS, D))
```

```python
import jax
import jax.numpy as jnp
from jax import lax
from jax.sharding import PartitionSpec as P

SLICES = 4
CAP = 2

contract_last = (((1,), (1,)), ((), ()))
contract_first = (((0,), (0,)), ((), ()))


def silu_parts(values_in):
    sigmoid_of = jax.nn.sigmoid(values_in)
    return (values_in * sigmoid_of, sigmoid_of * (1.0 + values_in * (1.0 - sigmoid_of)))


def half_swap(block, count, parity):
    half = count // 2
    route = [(c, (c + half) % count) for c in range(count) if c % 2 == parity]
    return lax.ppermute(block, "expert", route)


def three_parts(gates):
    first = lax.reduce_precision(gates, 8, 7)
    rest = gates - first
    second = lax.reduce_precision(rest, 8, 7)
    third = rest - second
    return [part.astype(jnp.bfloat16) for part in (first, second, third)]


def block_rank(hits, tok_dev):
    grouped = hits.reshape(hits.shape[0], -1, tok_dev)
    earlier = jnp.arange(tok_dev)[:, None] > jnp.arange(tok_dev)[None, :]
    ranks = jnp.sum(jnp.where(earlier[None, None], grouped[:, :, None, :], 0), axis=-1)
    return ranks.reshape(hits.shape)


def per_device(tokens, upstream, expert_ids, gates, relocate, w_gate_up, w_down):
    n_rows = lax.axis_size("dp")
    n_cols = lax.axis_size("expert")
    slots = n_rows // SLICES
    experts = slots * n_cols
    tok_dev, width = tokens.shape
    top = expert_ids.shape[1]
    slice_width = w_down.shape[2]
    half = n_cols // 2
    col = lax.axis_index("expert")
    slot_here = lax.axis_index("dp") // SLICES
    y_groups = [[x * SLICES + y for y in range(SLICES)] for x in range(slots)]
    x_groups = [[x * SLICES + y for x in range(slots)] for y in range(SLICES)]

    own_pack = jnp.concatenate([w_gate_up[0, 0], w_down[0, 0]], axis=0)
    far_pack = half_swap(own_pack, n_cols, 0)

    meta = jnp.concatenate(
        [expert_ids.astype(jnp.bfloat16)] + three_parts(gates)
        + [jnp.zeros((tok_dev, 128 - 4 * top), jnp.bfloat16)],
        axis=1,
    )
    packed = jnp.concatenate([tokens, upstream, meta], axis=1)
    gathered = lax.all_gather(packed, "expert", axis=0, tiled=True)

    even = col % 2 == 0
    rel_row = jnp.sum(
        jnp.where(jnp.arange(n_cols)[:, None] == col, relocate, 0), axis=0
    )
    served = jnp.where(even, (col + half * rel_row) % n_cols, col) * slots + jnp.arange(slots)
    meta_all = gathered[:, 2 * width :].astype(jnp.float32)
    ids_all = meta_all[:, :top].astype(jnp.int32)
    gates_all = (
        meta_all[:, top : 2 * top] + meta_all[:, 2 * top : 3 * top] + meta_all[:, 3 * top : 4 * top]
    )
    match = ids_all[None] == served[:, None, None]
    hits = jnp.sum(match.astype(jnp.int32), axis=-1)
    gate_of = jnp.sum(jnp.where(match, gates_all[None], 0.0), axis=-1)
    n_tok = ids_all.shape[0]
    place = CAP * (jnp.arange(n_tok, dtype=jnp.int32) // tok_dev)[None] + block_rank(hits, tok_dev)
    seats = n_cols * CAP
    seat = (hits[:, None, :] > 0) & (
        place[:, None, :] == jnp.arange(seats, dtype=jnp.int32)[None, :, None]
    )
    select = seat.reshape(slots * seats, n_tok).astype(jnp.bfloat16)
    rows = jnp.dot(select, gathered[:, : 2 * width], preferred_element_type=jnp.float32)
    gate_rows = jnp.sum(jnp.where(seat, gate_of[:, None, :], 0.0), axis=-1).reshape(-1, 1)
    sent = jnp.concatenate(
        [rows[:, :width].astype(jnp.bfloat16), (gate_rows * rows[:, width:]).astype(jnp.bfloat16)], axis=1
    )

    at_x = lax.all_to_all(
        sent, "dp", split_axis=0, concat_axis=0, axis_index_groups=x_groups, tiled=True
    )
    all_rows = lax.all_gather(at_x, "dp", axis=0, axis_index_groups=y_groups, tiled=True)
    rows_x = all_rows[:, :width]
    rows_d = all_rows[:, width:]

    rel_here = jnp.sum(jnp.where(jnp.arange(slots) == slot_here, rel_row, 0))
    pack = jnp.where(even & (rel_here == 1), far_pack, own_pack)
    gate_up = pack[: 2 * slice_width]
    down_rows = pack[2 * slice_width :]
    gate_and_up = lax.dot_general(
        rows_x, gate_up, contract_last, preferred_element_type=jnp.float32
    )
    gate_pre = gate_and_up[:, :slice_width]
    up_pre = gate_and_up[:, slice_width:]
    activated, slope_of = silu_parts(gate_pre)
    hidden = (activated * up_pre).astype(jnp.bfloat16)
    hidden_grad = lax.dot_general(
        rows_d, down_rows, contract_last, preferred_element_type=jnp.float32
    )
    pre_grads = jnp.concatenate(
        [
            (hidden_grad * up_pre * slope_of).astype(jnp.bfloat16),
            (hidden_grad * activated).astype(jnp.bfloat16),
        ],
        axis=1,
    )
    slice_part = jnp.dot(pre_grads, gate_up, preferred_element_type=jnp.float32).astype(
        jnp.bfloat16
    )
    grad_gu = lax.dot_general(
        pre_grads, rows_x, contract_first, preferred_element_type=jnp.float32
    ).astype(jnp.bfloat16)
    grad_dn = lax.dot_general(
        hidden, rows_d, contract_first, preferred_element_type=jnp.float32
    ).astype(jnp.bfloat16)
    grad_pack = jnp.concatenate([grad_gu, grad_dn], axis=0)
    far_grads = half_swap(grad_pack, n_cols, 1)
    grad_pack = jnp.where(~even & (rel_here == 1), far_grads, grad_pack)

    parts = lax.all_to_all(
        slice_part, "dp", split_axis=0, concat_axis=0, axis_index_groups=y_groups, tiled=True
    )
    summed = jnp.sum(
        parts.reshape(SLICES, slots * seats, width).astype(jnp.float32), axis=0
    ).astype(jnp.bfloat16)
    back = lax.all_to_all(
        summed, "dp", split_axis=0, concat_axis=0, axis_index_groups=x_groups, tiled=True
    )
    partial = lax.dot_general(select, back, contract_first, preferred_element_type=jnp.float32)
    grad_tokens = lax.psum_scatter(
        partial, "expert", scatter_dimension=0, tiled=True
    ).astype(jnp.bfloat16)
    return (
        grad_tokens,
        grad_pack[: 2 * slice_width].reshape(w_gate_up.shape),
        grad_pack[2 * slice_width :].reshape(w_down.shape),
    )


def solution(mesh):
    return jax.shard_map(
        per_device,
        mesh=mesh,
        in_specs=(
            P(("dp", "expert"), None),
            P(("dp", "expert"), None),
            P(("dp", "expert"), None),
            P(("dp", "expert"), None),
            P(),
            P("expert", "dp", None, None),
            P("expert", "dp", None, None),
        ),
        out_specs=(
            P(("dp", "expert"), None),
            P("expert", "dp", None, None),
            P("expert", "dp", None, None),
        ),
        check_vma=False,
    )
```

```python
import functools

import jax
import jax.numpy as jnp
from jax import lax
from jax.experimental import pallas as pl
from jax.experimental.pallas import tpu as pltpu
from jax.sharding import PartitionSpec as P

SLICES = 4
CAP = 2
MESH = pl.DeviceIdType.MESH

contract_last = (((1,), (1,)), ((), ()))
contract_first = (((0,), (0,)), ((), ()))
VMEM_SPEC = pl.BlockSpec(memory_space=pltpu.VMEM)


def silu_parts(values_in):
    sigmoid_of = jax.nn.sigmoid(values_in)
    return (values_in * sigmoid_of, sigmoid_of * (1.0 + values_in * (1.0 - sigmoid_of)))


def half_swap(block, count, parity):
    half = count // 2
    route = [(c, (c + half) % count) for c in range(count) if c % 2 == parity]
    return lax.ppermute(block, "expert", route)


def three_parts(gates):
    first = lax.reduce_precision(gates, 8, 7)
    rest = gates - first
    second = lax.reduce_precision(rest, 8, 7)
    third = rest - second
    return [part.astype(jnp.bfloat16) for part in (first, second, third)]


def block_rank(hits, tok_dev):
    grouped = hits.reshape(hits.shape[0], -1, tok_dev)
    earlier = jnp.arange(tok_dev)[:, None] > jnp.arange(tok_dev)[None, :]
    ranks = jnp.sum(jnp.where(earlier[None, None], grouped[:, :, None, :], 0), axis=-1)
    return ranks.reshape(hits.shape)


def meet(peers):
    barrier = pltpu.get_barrier_semaphore()
    for peer in peers:
        pl.semaphore_signal(barrier, inc=1, device_id=peer, device_id_type=MESH)
    pl.semaphore_wait(barrier, len(peers))


def remote(src, dst, send_sem, recv_sem, peer):
    return pltpu.make_async_remote_copy(
        src_ref=src, dst_ref=dst, send_sem=send_sem, recv_sem=recv_sem,
        device_id=peer, device_id_type=MESH,
    )


def gather_kernel(n_cols, own_ref, all_ref, keep_sem, send_p, recv_p, send_m, recv_m, send_s, recv_s):
    e = lax.axis_index("expert")
    chips = n_cols // 2
    ahead = {"expert": lax.rem(e + 2, n_cols)}
    behind = {"expert": lax.rem(e + n_cols - 2, n_cols)}
    twin = {"expert": e + 1 - 2 * lax.rem(e, 2)}
    meet([ahead, behind, twin])
    up_steps, down_steps = chips // 2, chips // 2 - 1
    parts = own_ref.shape[0]

    def slot(shift, h):
        return parts * lax.rem(e + 2 * shift + n_cols, n_cols) + h

    def up(s, h, src):
        return remote(src, all_ref.at[slot(-s, h)], send_p.at[s, h], recv_p.at[s, h], ahead)

    def down(s, h, src):
        return remote(src, all_ref.at[slot(s, h)], send_m.at[s, h], recv_m.at[s, h], behind)

    def side(shift, h, src):
        index = shift % chips
        return remote(src, all_ref.at[slot(shift, h)], send_s.at[index, h], recv_s.at[index, h], twin)

    started = []
    keeps = []
    for h in range(parts):
        for copy in (up(0, h, own_ref.at[h]), down(0, h, own_ref.at[h]), side(0, h, own_ref.at[h])):
            copy.start()
            started.append(copy)
        keep = pltpu.make_async_copy(own_ref.at[h], all_ref.at[slot(0, h)], keep_sem.at[h])
        keep.start()
        keeps.append(keep)
    for s in range(1, up_steps + 1):
        for h in range(parts):
            block = all_ref.at[slot(-s, h)]
            up(s - 1, h, block).wait_recv()
            if s < up_steps:
                copy = up(s, h, block)
                copy.start()
                started.append(copy)
            copy = side(-s, h, block)
            copy.start()
            started.append(copy)
            if s <= down_steps:
                block = all_ref.at[slot(s, h)]
                down(s - 1, h, block).wait_recv()
                if s < down_steps:
                    copy = down(s, h, block)
                    copy.start()
                    started.append(copy)
                copy = side(s, h, block)
                copy.start()
                started.append(copy)
    for shift in range(-up_steps, down_steps + 1):
        for h in range(parts):
            other = parts * lax.rem(e + 1 - 2 * lax.rem(e, 2) + 2 * shift + n_cols, n_cols) + h
            index = shift % chips
            remote(all_ref.at[other], all_ref.at[other], send_s.at[index, h], recv_s.at[index, h], twin).wait_recv()
    for copy in started:
        copy.wait_send()
    for keep in keeps:
        keep.wait()


def gather_tokens(packed, n_cols):
    parts, rows, width = packed.shape
    chips = n_cols // 2
    up, down = chips // 2, chips // 2 - 1
    dma = pltpu.SemaphoreType.DMA
    return pl.pallas_call(
        functools.partial(gather_kernel, n_cols),
        out_shape=jax.ShapeDtypeStruct((n_cols * parts, rows, width), packed.dtype),
        in_specs=[VMEM_SPEC],
        out_specs=VMEM_SPEC,
        scratch_shapes=[
            dma((parts,)), dma((up, parts)), dma((up, parts)), dma((down, parts)), dma((down, parts)),
            dma((chips, parts)), dma((chips, parts)),
        ],
        compiler_params=pltpu.CompilerParams(collective_id=0, has_side_effects=True),
        name="gather_tokens",
    )(packed)


def xy_peers():
    row = lax.axis_index("dp")
    my_x, my_y = row // SLICES, lax.rem(row, SLICES)

    def at(dx, dy):
        return {"dp": lax.rem(my_x + dx, SLICES) * SLICES + lax.rem(my_y + dy, SLICES)}

    return my_x, my_y, at


def dispatch_kernel(sent_ref, all_ref, keep_sem, send_x, recv_x, send_y, recv_y, send_f, recv_f):
    my_x, my_y, at = xy_peers()
    north, south = at(0, 1), at(0, 3)
    meet([at(1, 0), at(2, 0), at(3, 0), north, south])
    half = sent_ref.shape[1] // 2
    low, high = pl.ds(0, half), pl.ds(half, half)
    x_of = [lax.rem(my_x + k, SLICES) for k in range(SLICES)]
    y_of = [lax.rem(my_y + k, SLICES) for k in range(SLICES)]
    started = []

    def go(copy):
        copy.start()
        started.append(copy)

    keep = pltpu.make_async_copy(sent_ref.at[my_x], all_ref.at[my_y, my_x], keep_sem)
    keep.start()

    def x_copy(k):
        return remote(
            sent_ref.at[x_of[k]], all_ref.at[my_y, my_x], send_x.at[SLICES - k], recv_x.at[SLICES - k], at(k, 0)
        )

    def y_send(k, src):
        block = all_ref.at[my_y, x_of[k]]
        go(remote(src, block, send_y.at[0, k], recv_y.at[0, k], north))
        go(remote(src, block, send_y.at[1, k], recv_y.at[1, k], south))

    def x_then_y(k):
        block = all_ref.at[my_y, x_of[k]]
        remote(block, block, send_x.at[k], recv_x.at[k], at(k, 0)).wait_recv()
        y_send(k, block)

    def pass_on(k):
        block = all_ref.at[y_of[3], x_of[k]]
        remote(block, block, send_y.at[0, k], recv_y.at[0, k], south).wait_recv()
        part = all_ref.at[y_of[3], x_of[k], low]
        go(remote(part, part, send_f.at[0, k], recv_f.at[0, k], north))
        block = all_ref.at[y_of[1], x_of[k]]
        remote(block, block, send_y.at[1, k], recv_y.at[1, k], north).wait_recv()
        part = all_ref.at[y_of[1], x_of[k], high]
        go(remote(part, part, send_f.at[1, k], recv_f.at[1, k], south))

    y_send(0, sent_ref.at[my_x])
    for k in (1, 3, 2):
        go(x_copy(k))
    x_then_y(1)
    x_then_y(3)
    pass_on(0)
    x_then_y(2)
    pass_on(1)
    pass_on(3)
    pass_on(2)
    for k in range(SLICES):
        part = all_ref.at[y_of[2], x_of[k], low]
        remote(part, part, send_f.at[0, k], recv_f.at[0, k], south).wait_recv()
        part = all_ref.at[y_of[2], x_of[k], high]
        remote(part, part, send_f.at[1, k], recv_f.at[1, k], north).wait_recv()
    for copy in started:
        copy.wait_send()
    keep.wait()


def dispatch_rows(sent):
    slots, seats, width = sent.shape
    dma = pltpu.SemaphoreType.DMA
    return pl.pallas_call(
        dispatch_kernel,
        out_shape=jax.ShapeDtypeStruct((SLICES, slots, seats, width), sent.dtype),
        in_specs=[VMEM_SPEC],
        out_specs=VMEM_SPEC,
        scratch_shapes=[
            dma, dma((SLICES,)), dma((SLICES,)), dma((2, SLICES)), dma((2, SLICES)), dma((2, SLICES)), dma((2, SLICES)),
        ],
        compiler_params=pltpu.CompilerParams(collective_id=1, has_side_effects=True),
        cost_estimate=pl.CostEstimate(flops=0, bytes_accessed=150_000_000, transcendentals=0),
        name="dispatch_rows",
    )(sent)


def return_kernel(
    part_ref, back_ref, relay, summed, got, total,
    send_r, recv_r, send_d, recv_d, send_t, recv_t, send_x, recv_x, keep_sem,
):
    my_x, my_y, at = xy_peers()
    north, south = at(0, 1), at(0, 3)
    meet([at(1, 0), at(2, 0), at(3, 0), north, south])
    y_of = [lax.rem(my_y + k, SLICES) for k in range(SLICES)]
    pair = SLICES // 2
    started = []

    def go(copy):
        copy.start()
        started.append(copy)

    def relay_copy(way, i):
        block = pair * (1 - way) + i
        return remote(
            part_ref.at[y_of[2], block], relay.at[way, i], send_r.at[way, i], recv_r.at[way, i], (north, south)[way]
        )

    def direct_copy(way, i):
        block = pair * way + i
        return remote(
            part_ref.at[y_of[1 if way == 0 else 3], block], got.at[way, block],
            send_d.at[way, i], recv_d.at[way, i], (north, south)[way],
        )

    def total_copy(way, i):
        block = pair * (1 - way) + i
        return remote(
            summed.at[way, i], got.at[way, block], send_t.at[way, i], recv_t.at[way, i], (north, south)[way]
        )

    for i in range(pair):
        for way in range(2):
            go(relay_copy(way, i))
    for i in range(pair):
        for way in range(2):
            go(direct_copy(way, i))
    for i in range(pair):
        for way in range(2):
            relay_copy(way, i).wait_recv()
            block = pair * (1 - way) + i
            mine = part_ref[y_of[1 if way == 0 else 3], block].astype(jnp.float32)
            summed[way, i] = (mine + relay[way, i].astype(jnp.float32)).astype(jnp.bfloat16)
            go(total_copy(way, i))
    for i in range(pair):
        for way in range(2):
            direct_copy(way, i).wait_recv()
            total_copy(way, i).wait_recv()
    for k in (2, 1, 3, 0):
        block = lax.rem(my_x + k, SLICES)
        total[block] = (
            part_ref[my_y, block].astype(jnp.float32)
            + got[0, block].astype(jnp.float32)
            + got[1, block].astype(jnp.float32)
        ).astype(jnp.bfloat16)
        if k > 0:
            go(remote(
                total.at[block], back_ref.at[my_x], send_x.at[SLICES - k], recv_x.at[SLICES - k], at(k, 0)
            ))
        else:
            keep = pltpu.make_async_copy(total.at[block], back_ref.at[my_x], keep_sem)
            keep.start()
            keep.wait()
    for k in (1, 3, 2):
        block = back_ref.at[lax.rem(my_x + k, SLICES)]
        remote(block, block, send_x.at[k], recv_x.at[k], at(k, 0)).wait_recv()
    for copy in started:
        copy.wait_send()


def return_rows(parts):
    _, slots, seats, width = parts.shape
    dma = pltpu.SemaphoreType.DMA
    pair = SLICES // 2
    return pl.pallas_call(
        return_kernel,
        out_shape=jax.ShapeDtypeStruct((slots, seats, width), parts.dtype),
        in_specs=[VMEM_SPEC],
        out_specs=VMEM_SPEC,
        scratch_shapes=[
            pltpu.VMEM((2, pair, seats, width), jnp.bfloat16),
            pltpu.VMEM((2, pair, seats, width), jnp.bfloat16),
            pltpu.VMEM((2, slots, seats, width), jnp.bfloat16),
            pltpu.VMEM((slots, seats, width), jnp.bfloat16),
        ] + [dma((2, pair))] * 6 + [dma((SLICES,))] * 2 + [dma],
        compiler_params=pltpu.CompilerParams(collective_id=2, has_side_effects=True),
        cost_estimate=pl.CostEstimate(flops=0, bytes_accessed=100_000_000, transcendentals=0),
        name="return_rows",
    )(parts)


def home_kernel(n_cols, rows_ref, home_ref, send_sem, recv_sem, keep_sem):
    e = lax.axis_index("expert")
    peers = [{"expert": lax.rem(e + k, n_cols)} for k in range(n_cols)]
    meet(peers[1:])
    order = sorted(range(1, n_cols), key=lambda k: -min(k, n_cols - k))
    for k in order:
        remote(
            rows_ref.at[lax.rem(e + k, n_cols)], home_ref.at[e], send_sem.at[k], recv_sem.at[k], peers[k]
        ).start()
    keep = pltpu.make_async_copy(rows_ref.at[e], home_ref.at[e], keep_sem)
    keep.start()
    keep.wait()
    for k in order:
        block = home_ref.at[lax.rem(e + n_cols - k, n_cols)]
        remote(block, block, send_sem.at[k], recv_sem.at[k], peers[k]).wait()


def bring_home(rows):
    n_cols = rows.shape[0]
    dma = pltpu.SemaphoreType.DMA
    return pl.pallas_call(
        functools.partial(home_kernel, n_cols),
        out_shape=jax.ShapeDtypeStruct(rows.shape, rows.dtype),
        in_specs=[VMEM_SPEC],
        out_specs=VMEM_SPEC,
        scratch_shapes=[dma((n_cols,)), dma((n_cols,)), dma],
        compiler_params=pltpu.CompilerParams(collective_id=3, has_side_effects=True),
        cost_estimate=pl.CostEstimate(flops=0, bytes_accessed=100_000_000, transcendentals=0),
        name="bring_home",
    )(rows)


def per_device(tokens, upstream, expert_ids, gates, relocate, w_gate_up, w_down):
    n_rows = lax.axis_size("dp")
    n_cols = lax.axis_size("expert")
    slots = n_rows // SLICES
    tok_dev, width = tokens.shape
    top = expert_ids.shape[1]
    slice_width = w_down.shape[2]
    half = n_cols // 2
    seats = n_cols * CAP
    col = lax.axis_index("expert")
    slot_here = lax.axis_index("dp") // SLICES

    meta = jnp.concatenate(
        [expert_ids.astype(jnp.bfloat16)] + three_parts(gates)
        + [jnp.zeros((tok_dev, 128 - 4 * top), jnp.bfloat16)],
        axis=1,
    )
    packed = jnp.concatenate([tokens, upstream, meta], axis=1)
    gathered = gather_tokens(packed.reshape(2, tok_dev // 2, -1), n_cols)

    own_pack = jnp.concatenate([w_gate_up[0, 0], w_down[0, 0]], axis=0)
    gathered, own_pack = lax.optimization_barrier((gathered, own_pack))
    far_pack = half_swap(own_pack, n_cols, 0)
    gathered = gathered.reshape(n_cols * tok_dev, -1)

    even = col % 2 == 0
    rel_row = jnp.sum(
        jnp.where(jnp.arange(n_cols)[:, None] == col, relocate, 0), axis=0
    )
    served = jnp.where(even, (col + half * rel_row) % n_cols, col) * slots + jnp.arange(slots)
    meta_all = gathered[:, 2 * width :].astype(jnp.float32)
    ids_all = meta_all[:, :top].astype(jnp.int32)
    gates_all = (
        meta_all[:, top : 2 * top] + meta_all[:, 2 * top : 3 * top] + meta_all[:, 3 * top : 4 * top]
    )
    match = ids_all[None] == served[:, None, None]
    hits = jnp.sum(match.astype(jnp.int32), axis=-1)
    gate_of = jnp.sum(jnp.where(match, gates_all[None], 0.0), axis=-1)
    n_tok = ids_all.shape[0]
    place = CAP * (jnp.arange(n_tok, dtype=jnp.int32) // tok_dev)[None] + block_rank(hits, tok_dev)
    seat = (hits[:, None, :] > 0) & (
        place[:, None, :] == jnp.arange(seats, dtype=jnp.int32)[None, :, None]
    )
    select = seat.reshape(slots * seats, n_tok).astype(jnp.bfloat16)
    rows = jnp.dot(select, gathered[:, : 2 * width], preferred_element_type=jnp.float32)
    gate_rows = jnp.sum(jnp.where(seat, gate_of[:, None, :], 0.0), axis=-1).reshape(-1, 1)
    sent = jnp.concatenate(
        [rows[:, :width].astype(jnp.bfloat16), (gate_rows * rows[:, width:]).astype(jnp.bfloat16)], axis=1
    )

    all_rows = dispatch_rows(sent.reshape(slots, seats, 2 * width)).reshape(-1, 2 * width)
    rows_x = all_rows[:, :width]
    rows_d = all_rows[:, width:]

    rel_here = jnp.sum(jnp.where(jnp.arange(slots) == slot_here, rel_row, 0))
    pack = jnp.where(even & (rel_here == 1), far_pack, own_pack)
    gate_up = pack[: 2 * slice_width]
    down_rows = pack[2 * slice_width :]
    gate_and_up = lax.dot_general(
        rows_x, gate_up, contract_last, preferred_element_type=jnp.float32
    )
    gate_pre = gate_and_up[:, :slice_width]
    up_pre = gate_and_up[:, slice_width:]
    activated, slope_of = silu_parts(gate_pre)
    hidden = (activated * up_pre).astype(jnp.bfloat16)
    hidden_grad = lax.dot_general(
        rows_d, down_rows, contract_last, preferred_element_type=jnp.float32
    )
    pre_grads = jnp.concatenate(
        [
            (hidden_grad * up_pre * slope_of).astype(jnp.bfloat16),
            (hidden_grad * activated).astype(jnp.bfloat16),
        ],
        axis=1,
    )
    slice_part = jnp.dot(pre_grads, gate_up, preferred_element_type=jnp.float32).astype(
        jnp.bfloat16
    )
    grad_gu = lax.dot_general(
        pre_grads, rows_x, contract_first, preferred_element_type=jnp.float32
    ).astype(jnp.bfloat16)
    grad_dn = lax.dot_general(
        hidden, rows_d, contract_first, preferred_element_type=jnp.float32
    ).astype(jnp.bfloat16)
    grad_pack = jnp.concatenate([grad_gu, grad_dn], axis=0)
    slice_part, grad_pack = lax.optimization_barrier((slice_part, grad_pack))
    far_grads = half_swap(grad_pack, n_cols, 1)
    grad_pack = jnp.where(~even & (rel_here == 1), far_grads, grad_pack)

    back = return_rows(slice_part.reshape(SLICES, slots, seats, width))
    rows_home = (
        back.reshape(slots, n_cols, CAP, width).transpose(1, 0, 2, 3).reshape(n_cols, slots * CAP, width)
    )
    home = bring_home(rows_home).reshape(n_cols * slots * CAP, width)

    flat_ids = expert_ids.reshape(-1)
    experts = slots * n_cols
    relocated = jnp.sum(
        jnp.where(flat_ids[:, None] == jnp.arange(experts)[None, :], relocate.reshape(1, experts), 0), axis=1
    )
    home_col = flat_ids // slots
    served_col = jnp.where(home_col % 2 == 0, (home_col + half * relocated) % n_cols, home_col)
    token_of = jnp.arange(flat_ids.shape[0], dtype=jnp.int32) // top
    earlier = (flat_ids[:, None] == flat_ids[None, :]) & (token_of[None, :] < token_of[:, None])
    rank = jnp.sum(earlier.astype(jnp.int32), axis=1)
    target = ((served_col * slots + flat_ids % slots) * CAP + rank).reshape(tok_dev, top)
    picks = jnp.sum(
        (target[:, :, None] == jnp.arange(home.shape[0], dtype=jnp.int32)[None, None, :]).astype(jnp.bfloat16),
        axis=1,
    )
    grad_tokens = jnp.dot(picks, home, preferred_element_type=jnp.float32).astype(jnp.bfloat16)
    return (
        grad_tokens,
        grad_pack[: 2 * slice_width].reshape(w_gate_up.shape),
        grad_pack[2 * slice_width :].reshape(w_down.shape),
    )


def solution(mesh):
    return jax.shard_map(
        per_device,
        mesh=mesh,
        in_specs=(
            P(("dp", "expert"), None),
            P(("dp", "expert"), None),
            P(("dp", "expert"), None),
            P(("dp", "expert"), None),
            P(),
            P("expert", "dp", None, None),
            P("expert", "dp", None, None),
        ),
        out_specs=(
            P(("dp", "expert"), None),
            P("expert", "dp", None, None),
            P("expert", "dp", None, None),
        ),
        check_vma=False,
    )
```

```python
import functools

import jax
import jax.numpy as jnp
from jax import lax
from jax.experimental import pallas as pl
from jax.experimental.pallas import tpu as pltpu
from jax.sharding import PartitionSpec as P

SLICES = 4
CAP = 2
MESH = pl.DeviceIdType.MESH

contract_last = (((1,), (1,)), ((), ()))
contract_first = (((0,), (0,)), ((), ()))
VMEM_SPEC = pl.BlockSpec(memory_space=pltpu.VMEM)


def silu_parts(values_in):
    sigmoid_of = jax.nn.sigmoid(values_in)
    return (values_in * sigmoid_of, sigmoid_of * (1.0 + values_in * (1.0 - sigmoid_of)))


def half_swap(block, count, parity):
    half = count // 2
    route = [(c, (c + half) % count) for c in range(count) if c % 2 == parity]
    return lax.ppermute(block, "expert", route)


def three_parts(gates):
    first = lax.reduce_precision(gates, 8, 7)
    rest = gates - first
    second = lax.reduce_precision(rest, 8, 7)
    third = rest - second
    return [part.astype(jnp.bfloat16) for part in (first, second, third)]


def meet(peers):
    barrier = pltpu.get_barrier_semaphore()
    for peer in peers:
        pl.semaphore_signal(barrier, inc=1, device_id=peer, device_id_type=MESH)
    pl.semaphore_wait(barrier, len(peers))


def remote(src, dst, send_sem, recv_sem, peer):
    return pltpu.make_async_remote_copy(
        src_ref=src, dst_ref=dst, send_sem=send_sem, recv_sem=recv_sem,
        device_id=peer, device_id_type=MESH,
    )


def xy_peers():
    row = lax.axis_index("dp")
    my_x, my_y = row // SLICES, lax.rem(row, SLICES)

    def at(dx, dy):
        return {"dp": lax.rem(my_x + dx, SLICES) * SLICES + lax.rem(my_y + dy, SLICES)}

    return my_x, my_y, at


def near_order(chips):
    order = [0]
    for s in range(1, chips // 2):
        order += [s, -s]
    return order + [-(chips // 2)]


def pick_rows(block, lane_ids, row_ids, tok_dev, seats):
    n_tok, width = block.shape[0], (block.shape[1] - 128) // 2
    top = 8
    meta = block[:, 2 * width :].astype(jnp.float32)
    hit = meta[:, 0:1] == lane_ids
    for k in range(1, top):
        hit = hit | (meta[:, k : k + 1] == lane_ids)
    hits = jnp.where(hit, 1.0, 0.0)
    t_row = lax.broadcasted_iota(jnp.int32, (n_tok, n_tok), 0)
    t_col = lax.broadcasted_iota(jnp.int32, (n_tok, n_tok), 1)
    earlier = (t_row // tok_dev == t_col // tok_dev) & (t_col < t_row)
    ranks = jnp.dot(
        jnp.where(earlier, 1.0, 0.0).astype(jnp.bfloat16), hits.astype(jnp.bfloat16),
        preferred_element_type=jnp.float32,
    )
    device = (lax.broadcasted_iota(jnp.int32, hits.shape, 0) // tok_dev).astype(jnp.float32)
    seat = lax.rem(lax.broadcasted_iota(jnp.int32, hits.shape, 1), seats).astype(jnp.float32)
    chosen = hit & (CAP * device + ranks == seat)
    one_hot = jnp.where(chosen, 1.0, 0.0).astype(jnp.bfloat16)
    rows = lax.dot_general(one_hot, block, contract_first, preferred_element_type=jnp.float32)
    rows = rows[: row_ids.shape[0]]
    meta_rows = rows[:, 2 * width :]
    gates = sum(pltpu.roll(meta_rows, 128 - top * part, 1) for part in (1, 2, 3))
    lane = lax.broadcasted_iota(jnp.int32, meta_rows.shape, 1)
    gate = jnp.sum(
        jnp.where((lane < top) & (meta_rows == row_ids), gates, 0.0), axis=1, keepdims=True
    )
    return rows[:, :width].astype(jnp.bfloat16), (gate * rows[:, width : 2 * width]).astype(jnp.bfloat16)


def spread_kernel(
    n_cols, own_ref, lane_ref, row_ref, all_ref, held, sent, keep_sem,
    send_p, recv_p, send_m, recv_m, send_s, recv_s,
    keep_x, send_x, recv_x, send_y, recv_y, send_f, recv_f,
):
    e = lax.axis_index("expert")
    chips = n_cols // 2
    order = near_order(chips)
    my_x, my_y, at = xy_peers()
    north, south = at(0, 1), at(0, 3)
    ahead = {"expert": lax.rem(e + 2, n_cols)}
    behind = {"expert": lax.rem(e + n_cols - 2, n_cols)}
    twin = {"expert": e + 1 - 2 * lax.rem(e, 2)}
    tok_dev, full = own_ref.shape
    width = (full - 128) // 2
    groups, slots = sent.shape[0], sent.shape[1]
    seats = sent.shape[2]
    per_group = seats // CAP
    cuts = [pl.ds(0, width), pl.ds(width, width + 128)]
    up_steps, down_steps = chips // 2, chips // 2 - 1
    meet([ahead, behind, twin, at(1, 0), at(2, 0), at(3, 0), north, south])
    started = []

    def go(copy):
        copy.start()
        started.append(copy)

    def spot(shift, other, h):
        index = order.index(shift) * 2 + other
        return held.at[index // per_group, pl.ds(index % per_group * tok_dev, tok_dev), cuts[h]]

    def source(shift, h):
        return own_ref.at[:, cuts[h]] if shift == 0 else spot(shift, 0, h)

    def up(s, h):
        shift = -(s + 1)
        return remote(source(-s, h), spot(shift, 0, h), send_p.at[s, h], recv_p.at[s, h], ahead)

    def down(s, h):
        return remote(source(s, h), spot(s + 1, 0, h), send_m.at[s, h], recv_m.at[s, h], behind)

    def side(shift, h):
        index = order.index(shift)
        return remote(source(shift, h), spot(shift, 1, h), send_s.at[index, h], recv_s.at[index, h], twin)

    x_of = [lax.rem(my_x + k, SLICES) for k in range(SLICES)]
    y_of = [lax.rem(my_y + k, SLICES) for k in range(SLICES)]
    low, high = pl.ds(0, width), pl.ds(width, width)

    def x_copy(g, k):
        back = SLICES - k
        return remote(
            sent.at[g, x_of[k]], all_ref.at[g, my_y, my_x], send_x.at[g, back], recv_x.at[g, back], at(k, 0)
        )

    def y_send(g, k, src):
        block = all_ref.at[g, my_y, x_of[k]]
        go(remote(src, block, send_y.at[g, 0, k], recv_y.at[g, 0, k], north))
        go(remote(src, block, send_y.at[g, 1, k], recv_y.at[g, 1, k], south))

    def x_then_y(g):
        for k in (1, 3, 2):
            block = all_ref.at[g, my_y, x_of[k]]
            remote(block, block, send_x.at[g, k], recv_x.at[g, k], at(k, 0)).wait_recv()
            y_send(g, k, block)

    def pass_on(g):
        for k in (0, 1, 3, 2):
            block = all_ref.at[g, y_of[3], x_of[k]]
            remote(block, block, send_y.at[g, 0, k], recv_y.at[g, 0, k], south).wait_recv()
            part = all_ref.at[g, y_of[3], x_of[k], :, low]
            go(remote(part, part, send_f.at[g, 0, k], recv_f.at[g, 0, k], north))
            block = all_ref.at[g, y_of[1], x_of[k]]
            remote(block, block, send_y.at[g, 1, k], recv_y.at[g, 1, k], north).wait_recv()
            part = all_ref.at[g, y_of[1], x_of[k], :, high]
            go(remote(part, part, send_f.at[g, 1, k], recv_f.at[g, 1, k], south))

    def finish(g):
        for k in (0, 1, 3, 2):
            part = all_ref.at[g, y_of[2], x_of[k], :, low]
            remote(part, part, send_f.at[g, 0, k], recv_f.at[g, 0, k], south).wait_recv()
            part = all_ref.at[g, y_of[2], x_of[k], :, high]
            remote(part, part, send_f.at[g, 1, k], recv_f.at[g, 1, k], north).wait_recv()

    def choose(g):
        for index in range(g * per_group, (g + 1) * per_group):
            if index % 2 == 1:
                for h in range(2):
                    side(order[index // 2], h).wait_recv()
        block = held[g]
        x_rows, d_rows = pick_rows(block, lane_ref[0:1, :], row_ref[...], tok_dev, seats)
        for q in range(slots):
            sent[g, q, :, 0:width] = x_rows[q * seats : (q + 1) * seats]
            sent[g, q, :, width : 2 * width] = d_rows[q * seats : (q + 1) * seats]
        for k in (2, 1, 3):
            go(x_copy(g, k))
        y_send(g, 0, sent.at[g, my_x])
        keep = pltpu.make_async_copy(sent.at[g, my_x], all_ref.at[g, my_y, my_x], keep_x.at[g])
        keep.start()
        keeps.append(keep)

    keeps = []
    for h in range(2):
        go(up(0, h))
        go(down(0, h))
        go(side(0, h))
    own = pltpu.make_async_copy(own_ref, held.at[0, pl.ds(0, tok_dev)], keep_sem)
    own.start()
    own.wait()
    for s in range(1, up_steps + 1):
        for h in range(2):
            up(s - 1, h).wait_recv()
            if s < up_steps:
                go(up(s, h))
            if s <= down_steps:
                down(s - 1, h).wait_recv()
                if s < down_steps:
                    go(down(s, h))
        for h in range(2):
            go(side(-s, h))
            if s <= down_steps:
                go(side(s, h))
        if s % 2 == 0:
            choose(s // 2 - 1)
        elif s > 1:
            g = (s - 3) // 2
            x_then_y(g)
            if g > 0:
                pass_on(g - 1)
    last = groups - 1
    pass_on(last - 1)
    x_then_y(last)
    pass_on(last)
    for g in range(groups):
        finish(g)
    for copy in started:
        copy.wait_send()
    for keep in keeps:
        keep.wait()


def spread_rows(packed, lane_ids, row_ids, n_cols, slots):
    tok_dev, full = packed.shape
    chips = n_cols // 2
    groups = 4
    seats = n_cols * CAP // groups
    width = (full - 128) // 2
    up, down = chips // 2, chips // 2 - 1
    dma = pltpu.SemaphoreType.DMA
    return pl.pallas_call(
        functools.partial(spread_kernel, n_cols),
        out_shape=jax.ShapeDtypeStruct((groups, SLICES, slots, seats, 2 * width), packed.dtype),
        in_specs=[VMEM_SPEC] * 3,
        out_specs=VMEM_SPEC,
        scratch_shapes=[
            pltpu.VMEM((groups, n_cols // groups * tok_dev, full), packed.dtype),
            pltpu.VMEM((groups, slots, seats, 2 * width), packed.dtype),
            dma, dma((up, 2)), dma((up, 2)), dma((down, 2)), dma((down, 2)),
            dma((chips, 2)), dma((chips, 2)),
            dma((groups,)), dma((groups, SLICES)), dma((groups, SLICES)),
            dma((groups, 2, SLICES)), dma((groups, 2, SLICES)),
            dma((groups, 2, SLICES)), dma((groups, 2, SLICES)),
        ],
        compiler_params=pltpu.CompilerParams(collective_id=0, has_side_effects=True),
        cost_estimate=pl.CostEstimate(flops=0, bytes_accessed=200_000_000, transcendentals=0),
        name="spread_rows",
    )(packed, lane_ids, row_ids)


def return_kernel(
    part_ref, back_ref, relay, summed, got, total,
    send_r, recv_r, send_d, recv_d, send_t, recv_t, send_x, recv_x, keep_sem,
):
    my_x, my_y, at = xy_peers()
    north, south = at(0, 1), at(0, 3)
    meet([at(1, 0), at(2, 0), at(3, 0), north, south])
    y_of = [lax.rem(my_y + k, SLICES) for k in range(SLICES)]
    pair = SLICES // 2
    started = []

    def go(copy):
        copy.start()
        started.append(copy)

    def relay_copy(way, i):
        block = pair * (1 - way) + i
        return remote(
            part_ref.at[:, y_of[2], block], relay.at[way, i], send_r.at[way, i], recv_r.at[way, i], (north, south)[way]
        )

    def direct_copy(way, i):
        block = pair * way + i
        return remote(
            part_ref.at[:, y_of[1 if way == 0 else 3], block], got.at[way, block],
            send_d.at[way, i], recv_d.at[way, i], (north, south)[way],
        )

    def total_copy(way, i):
        block = pair * (1 - way) + i
        return remote(
            summed.at[way, i], got.at[way, block], send_t.at[way, i], recv_t.at[way, i], (north, south)[way]
        )

    for i in range(pair):
        for way in range(2):
            go(relay_copy(way, i))
    for i in range(pair):
        for way in range(2):
            go(direct_copy(way, i))
    for i in range(pair):
        for way in range(2):
            relay_copy(way, i).wait_recv()
            block = pair * (1 - way) + i
            mine = part_ref[:, y_of[1 if way == 0 else 3], block].astype(jnp.float32)
            summed[way, i] = (mine + relay[way, i].astype(jnp.float32)).astype(jnp.bfloat16)
            go(total_copy(way, i))
    for i in range(pair):
        for way in range(2):
            direct_copy(way, i).wait_recv()
            total_copy(way, i).wait_recv()
    for k in (2, 1, 3, 0):
        block = lax.rem(my_x + k, SLICES)
        total[block] = (
            part_ref[:, my_y, block].astype(jnp.float32)
            + got[0, block].astype(jnp.float32)
            + got[1, block].astype(jnp.float32)
        ).astype(jnp.bfloat16)
        if k > 0:
            go(remote(
                total.at[block], back_ref.at[my_x], send_x.at[SLICES - k], recv_x.at[SLICES - k], at(k, 0)
            ))
        else:
            keep = pltpu.make_async_copy(total.at[block], back_ref.at[my_x], keep_sem)
            keep.start()
            keep.wait()
    for k in (1, 3, 2):
        block = back_ref.at[lax.rem(my_x + k, SLICES)]
        remote(block, block, send_x.at[k], recv_x.at[k], at(k, 0)).wait_recv()
    for copy in started:
        copy.wait_send()


def return_rows(parts):
    groups, _, slots, seats, width = parts.shape
    dma = pltpu.SemaphoreType.DMA
    pair = SLICES // 2
    return pl.pallas_call(
        return_kernel,
        out_shape=jax.ShapeDtypeStruct((slots, groups, seats, width), parts.dtype),
        in_specs=[VMEM_SPEC],
        out_specs=VMEM_SPEC,
        scratch_shapes=[
            pltpu.VMEM((2, pair, groups, seats, width), jnp.bfloat16),
            pltpu.VMEM((2, pair, groups, seats, width), jnp.bfloat16),
            pltpu.VMEM((2, slots, groups, seats, width), jnp.bfloat16),
            pltpu.VMEM((slots, groups, seats, width), jnp.bfloat16),
        ] + [dma((2, pair))] * 6 + [dma((SLICES,))] * 2 + [dma],
        compiler_params=pltpu.CompilerParams(collective_id=2, has_side_effects=True),
        cost_estimate=pl.CostEstimate(flops=0, bytes_accessed=100_000_000, transcendentals=0),
        name="return_rows",
    )(parts)


def home_kernel(n_cols, rows_ref, home_ref, send_sem, recv_sem, keep_sem):
    e = lax.axis_index("expert")
    chips = n_cols // 2
    order = near_order(chips)
    chip, core = e // 2, lax.rem(e, 2)

    def peer(place):
        z = lax.rem(chip + order[place // 2] + chips, chips)
        return {"expert": 2 * z + (core if place % 2 == 0 else 1 - core)}

    def seen(place):
        shift = -order[place // 2]
        return order.index(shift if shift < chips // 2 else -shift) * 2 + place % 2

    meet([peer(place) for place in range(1, n_cols)])
    for place in reversed(range(1, n_cols)):
        remote(
            rows_ref.at[place], home_ref.at[seen(place)], send_sem.at[seen(place)], recv_sem.at[seen(place)], peer(place)
        ).start()
    keep = pltpu.make_async_copy(rows_ref.at[0], home_ref.at[0], keep_sem)
    keep.start()
    keep.wait()
    for place in range(1, n_cols):
        block = home_ref.at[place]
        remote(block, block, send_sem.at[place], recv_sem.at[place], peer(place)).wait()


def bring_home(rows):
    n_cols = rows.shape[0]
    dma = pltpu.SemaphoreType.DMA
    return pl.pallas_call(
        functools.partial(home_kernel, n_cols),
        out_shape=jax.ShapeDtypeStruct(rows.shape, rows.dtype),
        in_specs=[VMEM_SPEC],
        out_specs=VMEM_SPEC,
        scratch_shapes=[dma((n_cols,)), dma((n_cols,)), dma],
        compiler_params=pltpu.CompilerParams(collective_id=3, has_side_effects=True),
        cost_estimate=pl.CostEstimate(flops=0, bytes_accessed=100_000_000, transcendentals=0),
        name="bring_home",
    )(rows)


def per_device(tokens, upstream, expert_ids, gates, relocate, w_gate_up, w_down):
    n_rows = lax.axis_size("dp")
    n_cols = lax.axis_size("expert")
    slots = n_rows // SLICES
    tok_dev, width = tokens.shape
    top = expert_ids.shape[1]
    slice_width = w_down.shape[2]
    half = n_cols // 2
    seats = n_cols * CAP
    col = lax.axis_index("expert")
    slot_here = lax.axis_index("dp") // SLICES

    meta = jnp.concatenate(
        [expert_ids.astype(jnp.bfloat16)] + three_parts(gates)
        + [jnp.zeros((tok_dev, 128 - 4 * top), jnp.bfloat16)],
        axis=1,
    )
    packed = jnp.concatenate([tokens, upstream, meta], axis=1)
    own_pack = jnp.concatenate([w_gate_up[0, 0], w_down[0, 0]], axis=0)
    far_pack = half_swap(own_pack, n_cols, 0)

    even = col % 2 == 0
    rel_row = jnp.sum(
        jnp.where(jnp.arange(n_cols)[:, None] == col, relocate, 0), axis=0
    )
    served = jnp.where(even, (col + half * rel_row) % n_cols, col) * slots + jnp.arange(slots)
    group_seats = seats // 4
    lanes = jnp.arange(128, dtype=jnp.int32) // group_seats
    lane_ids = jnp.sum(
        jnp.where(lanes[None, :] == jnp.arange(slots)[:, None], served[:, None] + 1, 0), axis=0
    ) - 1
    lane_ids = lane_ids.astype(jnp.float32)
    row_ids = jnp.broadcast_to(lane_ids[: slots * group_seats, None], (slots * group_seats, 128))
    lane_ids = jnp.broadcast_to(lane_ids[None, :], (8, 128))
    spread = spread_rows(packed, lane_ids, row_ids, n_cols, slots)
    all_rows = spread.reshape(-1, 2 * width)
    rows_x = all_rows[:, :width]
    rows_d = all_rows[:, width:]

    rel_here = jnp.sum(jnp.where(jnp.arange(slots) == slot_here, rel_row, 0))
    pack = jnp.where(even & (rel_here == 1), far_pack, own_pack)
    gate_up = pack[: 2 * slice_width]
    down_rows = pack[2 * slice_width :]
    gate_and_up = lax.dot_general(
        rows_x, gate_up, contract_last, preferred_element_type=jnp.float32
    )
    gate_pre = gate_and_up[:, :slice_width]
    up_pre = gate_and_up[:, slice_width:]
    activated, slope_of = silu_parts(gate_pre)
    hidden = (activated * up_pre).astype(jnp.bfloat16)
    hidden_grad = lax.dot_general(
        rows_d, down_rows, contract_last, preferred_element_type=jnp.float32
    )
    pre_grads = jnp.concatenate(
        [
            (hidden_grad * up_pre * slope_of).astype(jnp.bfloat16),
            (hidden_grad * activated).astype(jnp.bfloat16),
        ],
        axis=1,
    )
    slice_part = jnp.dot(pre_grads, gate_up, preferred_element_type=jnp.float32).astype(
        jnp.bfloat16
    )
    grad_gu = lax.dot_general(
        pre_grads, rows_x, contract_first, preferred_element_type=jnp.float32
    ).astype(jnp.bfloat16)
    grad_dn = lax.dot_general(
        hidden, rows_d, contract_first, preferred_element_type=jnp.float32
    ).astype(jnp.bfloat16)
    grad_pack = jnp.concatenate([grad_gu, grad_dn], axis=0)
    slice_part, grad_pack = lax.optimization_barrier((slice_part, grad_pack))
    far_grads = half_swap(grad_pack, n_cols, 1)
    grad_pack = jnp.where(~even & (rel_here == 1), far_grads, grad_pack)

    back = return_rows(slice_part.reshape(*spread.shape[:-1], width))
    rows_home = (
        back.reshape(slots, n_cols, CAP, width).transpose(1, 0, 2, 3).reshape(n_cols, slots * CAP, width)
    )
    home = bring_home(rows_home).reshape(n_cols * slots * CAP, width)

    flat_ids = expert_ids.reshape(-1)
    experts = slots * n_cols
    relocated = jnp.sum(
        jnp.where(flat_ids[:, None] == jnp.arange(experts)[None, :], relocate.reshape(1, experts), 0), axis=1
    )
    home_col = flat_ids // slots
    served_col = jnp.where(home_col % 2 == 0, (home_col + half * relocated) % n_cols, home_col)
    token_of = jnp.arange(flat_ids.shape[0], dtype=jnp.int32) // top
    earlier = (flat_ids[:, None] == flat_ids[None, :]) & (token_of[None, :] < token_of[:, None])
    rank = jnp.sum(earlier.astype(jnp.int32), axis=1)
    chips = n_cols // 2
    shift = (served_col // 2 - col // 2 + chips // 2 + chips) % chips - chips // 2
    place = jnp.minimum(jnp.where(shift > 0, 2 * shift - 1, -2 * shift), chips - 1) * 2
    place = place + (served_col % 2 != col % 2).astype(jnp.int32)
    target = ((place * slots + flat_ids % slots) * CAP + rank).reshape(tok_dev, top)
    picks = jnp.sum(
        (target[:, :, None] == jnp.arange(home.shape[0], dtype=jnp.int32)[None, None, :]).astype(jnp.bfloat16),
        axis=1,
    )
    grad_tokens = jnp.dot(picks, home, preferred_element_type=jnp.float32).astype(jnp.bfloat16)
    return (
        grad_tokens,
        grad_pack[: 2 * slice_width].reshape(w_gate_up.shape),
        grad_pack[2 * slice_width :].reshape(w_down.shape),
    )


def solution(mesh):
    return jax.shard_map(
        per_device,
        mesh=mesh,
        in_specs=(
            P(("dp", "expert"), None),
            P(("dp", "expert"), None),
            P(("dp", "expert"), None),
            P(("dp", "expert"), None),
            P(),
            P("expert", "dp", None, None),
            P("expert", "dp", None, None),
        ),
        out_specs=(
            P(("dp", "expert"), None),
            P("expert", "dp", None, None),
            P("expert", "dp", None, None),
        ),
        check_vma=False,
    )
```

```python
import functools

import jax
import jax.numpy as jnp
from jax import lax
from jax.experimental import pallas as pl
from jax.experimental.pallas import tpu as pltpu
from jax.sharding import PartitionSpec as P

SLICES = 4
CAP = 2
MESH = pl.DeviceIdType.MESH

contract_last = (((1,), (1,)), ((), ()))
contract_first = (((0,), (0,)), ((), ()))
VMEM_SPEC = pl.BlockSpec(memory_space=pltpu.VMEM)


def silu_parts(values_in):
    sigmoid_of = jax.nn.sigmoid(values_in)
    return (values_in * sigmoid_of, sigmoid_of * (1.0 + values_in * (1.0 - sigmoid_of)))


def half_swap(block, count, parity):
    half = count // 2
    route = [(c, (c + half) % count) for c in range(count) if c % 2 == parity]
    return lax.ppermute(block, "expert", route)


def three_parts(gates):
    first = lax.reduce_precision(gates, 8, 7)
    rest = gates - first
    second = lax.reduce_precision(rest, 8, 7)
    third = rest - second
    return [part.astype(jnp.bfloat16) for part in (first, second, third)]


def meet(peers):
    barrier = pltpu.get_barrier_semaphore()
    for peer in peers:
        pl.semaphore_signal(barrier, inc=1, device_id=peer, device_id_type=MESH)
    pl.semaphore_wait(barrier, len(peers))


def remote(src, dst, send_sem, recv_sem, peer):
    return pltpu.make_async_remote_copy(
        src_ref=src, dst_ref=dst, send_sem=send_sem, recv_sem=recv_sem,
        device_id=peer, device_id_type=MESH,
    )


def xy_peers():
    row = lax.axis_index("dp")
    my_x, my_y = row // SLICES, lax.rem(row, SLICES)

    def at(dx, dy):
        return {"dp": lax.rem(my_x + dx, SLICES) * SLICES + lax.rem(my_y + dy, SLICES)}

    return my_x, my_y, at


def near_order(chips):
    order = [0]
    for s in range(1, chips // 2):
        order += [s, -s]
    return order + [-(chips // 2)]


def pick_rows(block, lane_ids, row_ids, tok_dev, seats):
    n_tok, width = block.shape[0], (block.shape[1] - 128) // 2
    top = 8
    meta = block[:, 2 * width :].astype(jnp.float32)
    hit = meta[:, 0:1] == lane_ids
    for k in range(1, top):
        hit = hit | (meta[:, k : k + 1] == lane_ids)
    hits = jnp.where(hit, 1.0, 0.0)
    t_row = lax.broadcasted_iota(jnp.int32, (n_tok, n_tok), 0)
    t_col = lax.broadcasted_iota(jnp.int32, (n_tok, n_tok), 1)
    earlier = (t_row // tok_dev == t_col // tok_dev) & (t_col < t_row)
    ranks = jnp.dot(
        jnp.where(earlier, 1.0, 0.0).astype(jnp.bfloat16), hits.astype(jnp.bfloat16),
        preferred_element_type=jnp.float32,
    )
    device = (lax.broadcasted_iota(jnp.int32, hits.shape, 0) // tok_dev).astype(jnp.float32)
    seat = lax.rem(lax.broadcasted_iota(jnp.int32, hits.shape, 1), seats).astype(jnp.float32)
    chosen = hit & (CAP * device + ranks == seat)
    one_hot = jnp.where(chosen, 1.0, 0.0).astype(jnp.bfloat16)
    rows = lax.dot_general(one_hot, block, contract_first, preferred_element_type=jnp.float32)
    rows = rows[: row_ids.shape[0]]
    meta_rows = rows[:, 2 * width :]
    gates = sum(pltpu.roll(meta_rows, 128 - top * part, 1) for part in (1, 2, 3))
    lane = lax.broadcasted_iota(jnp.int32, meta_rows.shape, 1)
    gate = jnp.sum(
        jnp.where((lane < top) & (meta_rows == row_ids), gates, 0.0), axis=1, keepdims=True
    )
    return rows[:, :width].astype(jnp.bfloat16), (gate * rows[:, width : 2 * width]).astype(jnp.bfloat16)


def moves_weights(e):
    return lax.rem(e, 2) == 0


def step_kernel(
    n_cols, own_ref, lane_ref, row_ref, flag_ref, picks_ref, gate_up_ref, down_ref,
    tokens_ref, grads_ref, far_grads,
    held, sent, rows_in, weights, far_weights, da_all, db_all, hidden_all,
    part_ref, relay, summed, got, total, back, places, home,
    keep_sem, send_p, recv_p, send_m, recv_m, send_s, recv_s,
    keep_x, send_x, recv_x, send_y, recv_y, send_f, recv_f,
    load_w, send_w, recv_w, send_g, recv_g,
    send_r, recv_r, send_d, recv_d, send_t, recv_t, send_b, recv_b, keep_b,
    send_h, recv_h, keep_h,
):
    e = lax.axis_index("expert")
    chips = n_cols // 2
    order = near_order(chips)
    chip, core = e // 2, lax.rem(e, 2)
    my_x, my_y, at = xy_peers()
    north, south = at(0, 1), at(0, 3)
    ahead = {"expert": lax.rem(e + 2, n_cols)}
    behind = {"expert": lax.rem(e + n_cols - 2, n_cols)}
    twin = {"expert": e + 1 - 2 * core}
    across = {"expert": lax.rem(e + chips, n_cols)}
    tok_dev, full = own_ref.shape
    width = (full - 128) // 2
    groups, slots = sent.shape[0], sent.shape[1]
    seats = sent.shape[2]
    block_rows = SLICES * slots * seats
    per_group = seats // CAP
    f_slice = down_ref.shape[0]
    quarter = width // 2
    cuts = [
        pl.ds(0, quarter), pl.ds(quarter, quarter), pl.ds(2 * quarter, quarter), pl.ds(3 * quarter, quarter + 128)
    ]
    n_cut = len(cuts)
    up_steps, down_steps = chips // 2, chips // 2 - 1
    early = moves_weights(e)

    def peer(place):
        z = lax.rem(chip + order[place // 2] + chips, chips)
        return {"expert": 2 * z + (core if place % 2 == 0 else 1 - core)}

    def seen(place):
        shift = -order[place // 2]
        return order.index(shift if shift < chips // 2 else -shift) * 2 + place % 2

    meet([peer(place) for place in range(1, n_cols)] + [at(1, 0), at(2, 0), at(3, 0), north, south])
    started = []

    def go(copy):
        copy.start()
        started.append(copy)

    def landed(ref, send_sem, recv_sem, who):
        remote(ref, ref, send_sem, recv_sem, who).wait_recv()

    def spot(shift, other, h):
        index = order.index(shift) * 2 + other
        return held.at[index // per_group, pl.ds(index % per_group * tok_dev, tok_dev), cuts[h]]

    def source(shift, h):
        return own_ref.at[:, cuts[h]] if shift == 0 else spot(shift, 0, h)

    def up(s, h):
        return remote(source(-s, h), spot(-(s + 1), 0, h), send_p.at[s, h], recv_p.at[s, h], ahead)

    def down(s, h):
        return remote(source(s, h), spot(s + 1, 0, h), send_m.at[s, h], recv_m.at[s, h], behind)

    def side(shift, h):
        index = order.index(shift)
        return remote(source(shift, h), spot(shift, 1, h), send_s.at[index, h], recv_s.at[index, h], twin)

    x_of = [lax.rem(my_x + k, SLICES) for k in range(SLICES)]
    y_of = [lax.rem(my_y + k, SLICES) for k in range(SLICES)]
    low, high = pl.ds(0, width), pl.ds(width, width)

    def x_copy(g, k):
        far = SLICES - k
        return remote(
            sent.at[g, x_of[k]], rows_in.at[g, my_y, my_x], send_x.at[g, far], recv_x.at[g, far], at(k, 0)
        )

    def y_send(g, k, src):
        block = rows_in.at[g, my_y, x_of[k]]
        go(remote(src, block, send_y.at[g, 0, k], recv_y.at[g, 0, k], north))
        go(remote(src, block, send_y.at[g, 1, k], recv_y.at[g, 1, k], south))

    def x_then_y(g):
        for k in (1, 3, 2):
            block = rows_in.at[g, my_y, x_of[k]]
            landed(block, send_x.at[g, k], recv_x.at[g, k], at(k, 0))
            y_send(g, k, block)

    def pass_on(g):
        for k in (0, 1, 3, 2):
            landed(rows_in.at[g, y_of[3], x_of[k]], send_y.at[g, 0, k], recv_y.at[g, 0, k], south)
            part = rows_in.at[g, y_of[3], x_of[k], :, low]
            go(remote(part, part, send_f.at[g, 0, k], recv_f.at[g, 0, k], north))
            landed(rows_in.at[g, y_of[1], x_of[k]], send_y.at[g, 1, k], recv_y.at[g, 1, k], north)
            part = rows_in.at[g, y_of[1], x_of[k], :, high]
            go(remote(part, part, send_f.at[g, 1, k], recv_f.at[g, 1, k], south))

    def finish(g):
        for k in (0, 1, 3, 2):
            landed(rows_in.at[g, y_of[2], x_of[k], :, low], send_f.at[g, 0, k], recv_f.at[g, 0, k], south)
            landed(rows_in.at[g, y_of[2], x_of[k], :, high], send_f.at[g, 1, k], recv_f.at[g, 1, k], north)

    keeps = []

    def choose(g):
        for index in range(g * per_group, (g + 1) * per_group):
            if index % 2 == 1:
                for h in range(n_cut):
                    side(order[index // 2], h).wait_recv()
        x_rows, d_rows = pick_rows(held[g], lane_ref[0:1, :], row_ref[...], tok_dev, seats)
        for q in range(slots):
            sent[g, q, :, 0:width] = x_rows[q * seats : (q + 1) * seats]
            sent[g, q, :, width : 2 * width] = d_rows[q * seats : (q + 1) * seats]
        for k in (2, 1, 3):
            go(x_copy(g, k))
        y_send(g, 0, sent.at[g, my_x])
        keep = pltpu.make_async_copy(sent.at[g, my_x], rows_in.at[g, my_y, my_x], keep_x.at[g])
        keep.start()
        keeps.append(keep)

    for h in range(n_cut):
        go(up(0, h))
        go(down(0, h))
        go(side(0, h))
    own = pltpu.make_async_copy(own_ref, held.at[0, pl.ds(0, tok_dev)], keep_sem)
    own.start()
    gate_up_at, down_at = pl.ds(0, 2 * f_slice), pl.ds(2 * f_slice, f_slice)
    loads = [
        pltpu.make_async_copy(gate_up_ref, weights.at[gate_up_at], load_w.at[0]),
        pltpu.make_async_copy(down_ref, weights.at[down_at], load_w.at[1]),
    ]
    for load in loads:
        load.start()
    own.wait()
    for s in range(1, up_steps + 1):
        for h in range(n_cut):
            up(s - 1, h).wait_recv()
            if s < up_steps:
                go(up(s, h))
            if s <= down_steps:
                down(s - 1, h).wait_recv()
                if s < down_steps:
                    go(down(s, h))
        for h in range(n_cut):
            go(side(-s, h))
            if s <= down_steps:
                go(side(s, h))
        if s == up_steps:
            w_copies = [
                remote(gate_up_ref, far_weights.at[gate_up_at], send_w.at[0], recv_w.at[0], across),
                remote(down_ref, far_weights.at[down_at], send_w.at[1], recv_w.at[1], across),
            ]

            @pl.when(early)
            def _():
                for copy in w_copies:
                    copy.start()

        if s % 2 == 0:
            choose(s // 2 - 1)
        elif s > 1:
            g = (s - 3) // 2
            x_then_y(g)
            if g > 0:
                pass_on(g - 1)
    last = groups - 1
    pass_on(last - 1)
    x_then_y(last)
    pass_on(last)
    for g in range(groups):
        finish(g)
    for keep in keeps:
        keep.wait()
    for load in loads:
        load.wait()

    @pl.when(early)
    def _():
        for copy in w_copies:
            copy.wait()
        moved = jnp.broadcast_to(flag_ref[0:1, 0:1], (f_slice, width)) > 0.5
        for i in range(3):
            at_rows = pl.ds(i * f_slice, f_slice)
            weights[at_rows] = jnp.where(
                moved, far_weights[at_rows].astype(jnp.float32), weights[at_rows].astype(jnp.float32)
            ).astype(jnp.bfloat16)

    w_gate, w_up, w_down = (pl.ds(i * f_slice, f_slice) for i in range(3))

    def x_and_d(g):
        block = rows_in[g].reshape(block_rows, 2 * width)
        return block[:, :width], block[:, width:]

    def forward(g, _):
        x, d = x_and_d(g)
        dot = functools.partial(lax.dot_general, dimension_numbers=contract_last, preferred_element_type=jnp.float32)
        up_pre = dot(x, weights[w_up])
        activated, slope_of = silu_parts(dot(x, weights[w_gate]))
        hidden_grad = dot(d, weights[w_down])
        hidden_all[g] = (activated * up_pre).astype(jnp.bfloat16)
        da_all[g] = (hidden_grad * up_pre * slope_of).astype(jnp.bfloat16)
        db_all[g] = (hidden_grad * activated).astype(jnp.bfloat16)
        return 0

    lax.fori_loop(0, groups, forward, 0)
    every_row = rows_in[...].reshape(groups * block_rows, 2 * width)
    g_copies = []
    for i, (left, lo) in enumerate(((da_all, 0), (db_all, 0), (hidden_all, width))):
        at_rows = pl.ds(i * f_slice, f_slice)
        grads_ref[at_rows] = lax.dot_general(
            left[...].reshape(groups * block_rows, f_slice), every_row[:, lo : lo + width], contract_first,
            preferred_element_type=jnp.float32,
        ).astype(jnp.bfloat16)
        g_copies.append(
            remote(grads_ref.at[at_rows], far_grads.at[at_rows], send_g.at[i], recv_g.at[i], across)
        )

    @pl.when(jnp.logical_not(early))
    def _():
        for copy in g_copies:
            copy.start()

    pair = SLICES // 2

    def relay_copy(g, way, i):
        block = pair * (1 - way) + i
        return remote(
            part_ref.at[g, y_of[2], block], relay.at[g, way, i], send_r.at[g, way, i], recv_r.at[g, way, i],
            (north, south)[way],
        )

    def direct_copy(g, way, i):
        block = pair * way + i
        return remote(
            part_ref.at[g, y_of[1 if way == 0 else 3], block], got.at[g, way, block],
            send_d.at[g, way, i], recv_d.at[g, way, i], (north, south)[way],
        )

    def total_copy(g, way, i):
        block = pair * (1 - way) + i
        return remote(
            summed.at[g, way, i], got.at[g, way, block], send_t.at[g, way, i], recv_t.at[g, way, i],
            (north, south)[way],
        )

    every = [(way, i) for i in range(pair) for way in range(2)]
    for g in range(groups):
        part = jnp.dot(
            da_all[g], weights[w_gate], preferred_element_type=jnp.float32
        ) + jnp.dot(db_all[g], weights[w_up], preferred_element_type=jnp.float32)
        part_ref[g] = part.astype(jnp.bfloat16).reshape(SLICES, slots, seats, width)
        for way, i in every:
            go(relay_copy(g, way, i))
        for way, i in every:
            go(direct_copy(g, way, i))
    for g in range(groups):
        for way, i in every:
            relay_copy(g, way, i).wait_recv()
            mine = part_ref[g, y_of[1 if way == 0 else 3], pair * (1 - way) + i].astype(jnp.float32)
            summed[g, way, i] = (mine + relay[g, way, i].astype(jnp.float32)).astype(jnp.bfloat16)
            go(total_copy(g, way, i))
    back_keeps = []

    per_place = slots * CAP
    n_rows = slots * seats
    to_row = lax.broadcasted_iota(jnp.int32, (n_rows, n_rows), 0)
    from_row = lax.broadcasted_iota(jnp.int32, (n_rows, n_rows), 1)
    wanted = (to_row % per_place) // CAP * seats + to_row // per_place * CAP + to_row % CAP
    regroup = jnp.where(from_row == wanted, 1.0, 0.0).astype(jnp.bfloat16)

    def send_home(g):
        for k in (1, 3, 2):
            landed(back.at[g, x_of[k]], send_b.at[g, k], recv_b.at[g, k], at(k, 0))
        back_keeps[g].wait()
        rows = jnp.dot(
            regroup, back[g].reshape(n_rows, width), preferred_element_type=jnp.float32
        ).astype(jnp.bfloat16)
        places[pl.ds(g * per_group, per_group)] = rows.reshape(per_group, per_place, width)
        for place in reversed(range(g * per_group, (g + 1) * per_group)):
            if place > 0:
                go(remote(
                    places.at[place], home.at[seen(place)], send_h.at[seen(place)], recv_h.at[seen(place)], peer(place)
                ))

    for g in range(groups):
        for way, i in every:
            direct_copy(g, way, i).wait_recv()
            total_copy(g, way, i).wait_recv()
        for k in (2, 1, 3, 0):
            block = x_of[k]
            total[g, block] = (
                part_ref[g, my_y, block].astype(jnp.float32)
                + got[g, 0, block].astype(jnp.float32)
                + got[g, 1, block].astype(jnp.float32)
            ).astype(jnp.bfloat16)
            if k > 0:
                far = SLICES - k
                go(remote(
                    total.at[g, block], back.at[g, my_x], send_b.at[g, far], recv_b.at[g, far], at(k, 0)
                ))
            else:
                keep = pltpu.make_async_copy(total.at[g, block], back.at[g, my_x], keep_b.at[g])
                keep.start()
                back_keeps.append(keep)
        if g > 0:
            send_home(g - 1)
    send_home(groups - 1)
    keep = pltpu.make_async_copy(places.at[0], home.at[0], keep_h)
    keep.start()
    keep.wait()
    for place in range(1, n_cols):
        landed(home.at[place], send_h.at[place], recv_h.at[place], peer(place))
    tokens_ref[...] = jnp.dot(
        picks_ref[...], home[...].reshape(n_cols * per_place, width), preferred_element_type=jnp.float32
    ).astype(tokens_ref.dtype)

    @pl.when(jnp.logical_not(early))
    def _():
        for copy in g_copies:
            copy.wait()

    for copy in started:
        copy.wait_send()


def whole_step(packed, lane_ids, row_ids, flag, picks, gate_up, down, n_cols, slots):
    tok_dev, full = packed.shape
    chips = n_cols // 2
    groups = 4
    seats = n_cols * CAP // groups
    width = (full - 128) // 2
    f_slice = down.shape[0]
    block_rows = SLICES * slots * seats
    pair = SLICES // 2
    up, down_steps = chips // 2, chips // 2 - 1
    cut = 4
    bf16 = jnp.bfloat16
    dma = pltpu.SemaphoreType.DMA
    any_spec = pl.BlockSpec(memory_space=pl.ANY)
    grads = jax.ShapeDtypeStruct((3 * f_slice, width), bf16)
    return pl.pallas_call(
        functools.partial(step_kernel, n_cols),
        out_shape=(jax.ShapeDtypeStruct((tok_dev, width), bf16), grads, grads),
        in_specs=[VMEM_SPEC] * 5 + [any_spec] * 2,
        out_specs=(VMEM_SPEC,) * 3,
        scratch_shapes=[
            pltpu.VMEM((groups, n_cols // groups * tok_dev, full), bf16),
            pltpu.VMEM((groups, slots, seats, 2 * width), bf16),
            pltpu.VMEM((groups, SLICES, slots, seats, 2 * width), bf16),
            pltpu.VMEM((3 * f_slice, width), bf16),
            pltpu.VMEM((3 * f_slice, width), bf16),
            pltpu.VMEM((groups, block_rows, f_slice), bf16),
            pltpu.VMEM((groups, block_rows, f_slice), bf16),
            pltpu.VMEM((groups, block_rows, f_slice), bf16),
            pltpu.VMEM((groups, SLICES, slots, seats, width), bf16),
            pltpu.VMEM((groups, 2, pair, seats, width), bf16),
            pltpu.VMEM((groups, 2, pair, seats, width), bf16),
            pltpu.VMEM((groups, 2, slots, seats, width), bf16),
            pltpu.VMEM((groups, slots, seats, width), bf16),
            pltpu.VMEM((groups, slots, seats, width), bf16),
            pltpu.VMEM((n_cols, slots * CAP, width), bf16),
            pltpu.VMEM((n_cols, slots * CAP, width), bf16),
            dma, dma((up, cut)), dma((up, cut)), dma((down_steps, cut)), dma((down_steps, cut)),
            dma((chips, cut)), dma((chips, cut)),
            dma((groups,)), dma((groups, SLICES)), dma((groups, SLICES)),
            dma((groups, 2, SLICES)), dma((groups, 2, SLICES)),
            dma((groups, 2, SLICES)), dma((groups, 2, SLICES)),
            dma((2,)), dma((2,)), dma((2,)), dma((3,)), dma((3,)),
        ] + [dma((groups, 2, pair))] * 6 + [
            dma((groups, SLICES)), dma((groups, SLICES)), dma((groups,)),
            dma((n_cols,)), dma((n_cols,)), dma,
        ],
        compiler_params=pltpu.CompilerParams(
            collective_id=0, has_side_effects=True, vmem_limit_bytes=56 * 1024 * 1024
        ),
        name="whole_step",
    )(packed, lane_ids, row_ids, flag, picks, gate_up, down)


def per_device(tokens, upstream, expert_ids, gates, relocate, w_gate_up, w_down):
    n_rows = lax.axis_size("dp")
    n_cols = lax.axis_size("expert")
    slots = n_rows // SLICES
    tok_dev, width = tokens.shape
    top = expert_ids.shape[1]
    slice_width = w_down.shape[2]
    half = n_cols // 2
    seats = n_cols * CAP
    col = lax.axis_index("expert")
    slot_here = lax.axis_index("dp") // SLICES

    meta = jnp.concatenate(
        [expert_ids.astype(jnp.bfloat16)] + three_parts(gates)
        + [jnp.zeros((tok_dev, 128 - 4 * top), jnp.bfloat16)],
        axis=1,
    )
    packed = jnp.concatenate([tokens, upstream, meta], axis=1)
    early = moves_weights(col)
    rel_row = jnp.sum(
        jnp.where(jnp.arange(n_cols)[:, None] == col, relocate, 0), axis=0
    )
    served = jnp.where(early, (col + half * rel_row) % n_cols, col) * slots + jnp.arange(slots)
    group_seats = seats // 4
    lanes = jnp.arange(128, dtype=jnp.int32) // group_seats
    lane_ids = jnp.sum(
        jnp.where(lanes[None, :] == jnp.arange(slots)[:, None], served[:, None] + 1, 0), axis=0
    ) - 1
    lane_ids = lane_ids.astype(jnp.float32)
    row_ids = jnp.broadcast_to(lane_ids[: slots * group_seats, None], (slots * group_seats, 128))
    lane_ids = jnp.broadcast_to(lane_ids[None, :], (8, 128))
    rel_here = jnp.sum(jnp.where(jnp.arange(slots) == slot_here, rel_row, 0))

    flat_ids = expert_ids.reshape(-1)
    experts = slots * n_cols
    relocated = jnp.sum(
        jnp.where(flat_ids[:, None] == jnp.arange(experts)[None, :], relocate.reshape(1, experts), 0), axis=1
    )
    home_col = flat_ids // slots
    served_col = jnp.where(moves_weights(home_col), (home_col + half * relocated) % n_cols, home_col)
    token_of = jnp.arange(flat_ids.shape[0], dtype=jnp.int32) // top
    earlier = (flat_ids[:, None] == flat_ids[None, :]) & (token_of[None, :] < token_of[:, None])
    rank = jnp.sum(earlier.astype(jnp.int32), axis=1)
    chips = n_cols // 2
    shift = (served_col // 2 - col // 2 + chips // 2 + chips) % chips - chips // 2
    place = jnp.minimum(jnp.where(shift > 0, 2 * shift - 1, -2 * shift), chips - 1) * 2
    place = place + (served_col % 2 != col % 2).astype(jnp.int32)
    target = ((place * slots + flat_ids % slots) * CAP + rank).reshape(tok_dev, top)
    n_home = n_cols * slots * CAP
    picks = jnp.sum(
        (target[:, :, None] == jnp.arange(n_home, dtype=jnp.int32)[None, None, :]).astype(jnp.bfloat16),
        axis=1,
    )
    flag = jnp.broadcast_to(rel_here.astype(jnp.float32), (8, 128))
    grad_tokens, near, far = whole_step(
        packed, lane_ids, row_ids, flag, picks, w_gate_up[0, 0], w_down[0, 0], n_cols, slots
    )
    came = ~early & (rel_here == 1)
    gate_up_rows = 2 * slice_width
    return (
        grad_tokens,
        jnp.where(came, far[:gate_up_rows], near[:gate_up_rows]).reshape(w_gate_up.shape),
        jnp.where(came, far[gate_up_rows:], near[gate_up_rows:]).reshape(w_down.shape),
    )


def solution(mesh):
    return jax.shard_map(
        per_device,
        mesh=mesh,
        in_specs=(
            P(("dp", "expert"), None),
            P(("dp", "expert"), None),
            P(("dp", "expert"), None),
            P(("dp", "expert"), None),
            P(),
            P("expert", "dp", None, None),
            P("expert", "dp", None, None),
        ),
        out_specs=(
            P(("dp", "expert"), None),
            P("expert", "dp", None, None),
            P("expert", "dp", None, None),
        ),
        check_vma=False,
    )
```

```python
import functools

import jax
import jax.numpy as jnp
from jax import lax
from jax.experimental import pallas as pl
from jax.experimental.pallas import tpu as pltpu
from jax.sharding import PartitionSpec as P

SLICES = 4
CAP = 2
MESH = pl.DeviceIdType.MESH

contract_last = (((1,), (1,)), ((), ()))
contract_first = (((0,), (0,)), ((), ()))
VMEM_SPEC = pl.BlockSpec(memory_space=pltpu.VMEM)


def silu_parts(values_in):
    sigmoid_of = jax.nn.sigmoid(values_in)
    return (values_in * sigmoid_of, sigmoid_of * (1.0 + values_in * (1.0 - sigmoid_of)))


def remote(src, dst, send_sem, recv_sem, peer):
    return pltpu.make_async_remote_copy(
        src_ref=src, dst_ref=dst, send_sem=send_sem, recv_sem=recv_sem,
        device_id=peer, device_id_type=MESH,
    )


def xy_peers():
    row = lax.axis_index("dp")
    my_x, my_y = row // SLICES, lax.rem(row, SLICES)

    def at(dx, dy):
        return {"dp": lax.rem(my_x + dx, SLICES) * SLICES + lax.rem(my_y + dy, SLICES)}

    return my_x, my_y, at


def near_order(chips):
    order = [0]
    for s in range(1, chips // 2):
        order += [s, -s]
    return order + [-(chips // 2)]


def pick_rows(block, lane_ids, row_ids, tok_dev, seats):
    n_tok, width = block.shape[0], (block.shape[1] - 128) // 2
    top = 8
    meta = block[:, 2 * width :].astype(jnp.float32)
    hit = meta[:, 0:1] == lane_ids
    for k in range(1, top):
        hit = hit | (meta[:, k : k + 1] == lane_ids)
    hits = jnp.where(hit, 1.0, 0.0)
    t_row = lax.broadcasted_iota(jnp.int32, (n_tok, n_tok), 0)
    t_col = lax.broadcasted_iota(jnp.int32, (n_tok, n_tok), 1)
    earlier = (t_row // tok_dev == t_col // tok_dev) & (t_col < t_row)
    ranks = jnp.dot(
        jnp.where(earlier, 1.0, 0.0).astype(jnp.bfloat16), hits.astype(jnp.bfloat16),
        preferred_element_type=jnp.float32,
    )
    device = (lax.broadcasted_iota(jnp.int32, hits.shape, 0) // tok_dev).astype(jnp.float32)
    seat = lax.rem(lax.broadcasted_iota(jnp.int32, hits.shape, 1), seats).astype(jnp.float32)
    chosen = hit & (CAP * device + ranks == seat)
    one_hot = jnp.where(chosen, 1.0, 0.0).astype(jnp.bfloat16)
    rows = lax.dot_general(one_hot, block, contract_first, preferred_element_type=jnp.float32)
    rows = rows[: row_ids.shape[0]]
    meta_rows = rows[:, 2 * width :]
    gates = sum(pltpu.roll(meta_rows, 128 - top * part, 1) for part in (1, 2, 3))
    lane = lax.broadcasted_iota(jnp.int32, meta_rows.shape, 1)
    gate = jnp.sum(
        jnp.where((lane < top) & (meta_rows == row_ids), gates, 0.0), axis=1, keepdims=True
    )
    return rows[:, :width].astype(jnp.bfloat16), (gate * rows[:, width : 2 * width]).astype(jnp.bfloat16)


def moves_weights(e):
    return (lax.rem(e, 2) == 0) & (lax.rem(e // 2, 4) < 3)


def step_kernel(
    n_cols, own_tokens, own_upstream, ids_ref, gates_ref, moves_ref, gate_up_ref, down_ref,
    tokens_ref, grad_gate_up_ref, grad_down_ref,
    own_ref, far_grads, held, sent, rows_in, weights, far_weights, da_all, db_all, hidden_all,
    part_ref, relay, summed, got, total, back, places, home,
    keep_sem, send_p2, recv_p2, send_p1, recv_p1, send_m2, recv_m2, send_m1, recv_m1, send_s, recv_s,
    keep_x, send_x, recv_x, send_y, recv_y, send_f, recv_f,
    load_w, send_w, recv_w, send_g, recv_g,
    send_r, recv_r, send_d, recv_d, send_t, recv_t, send_b, recv_b, keep_b,
    send_h, recv_h, keep_h,
):
    e = lax.axis_index("expert")
    chips = n_cols // 2
    order = near_order(chips)
    chip, core = e // 2, lax.rem(e, 2)
    my_x, my_y, at = xy_peers()
    north, south = at(0, 1), at(0, 3)
    ahead, behind = [
        [{"expert": lax.rem(e + sign * 2 * hops + n_cols, n_cols)} for hops in (1, 2)] for sign in (1, -1)
    ]
    twin = {"expert": e + 1 - 2 * core}
    across = {"expert": lax.rem(e + chips, n_cols)}
    tok_dev, full = own_ref.shape
    width = (full - 128) // 2
    groups, slots = sent.shape[0], sent.shape[1]
    seats = sent.shape[2]
    block_rows = SLICES * slots * seats
    per_group = seats // CAP
    f_slice = down_ref.shape[0]
    cuts = [pl.ds(0, width), pl.ds(width, width + 128)]
    n_cut = len(cuts)
    relays = chips // 4
    early = moves_weights(e)

    def peer(place):
        z = lax.rem(chip + order[place // 2] + chips, chips)
        return {"expert": 2 * z + (core if place % 2 == 0 else 1 - core)}

    def seen(place):
        shift = -order[place // 2]
        return order.index(shift if shift < chips // 2 else -shift) * 2 + place % 2

    peers = [peer(place) for place in range(1, n_cols)] + [at(1, 0), at(2, 0), at(3, 0), north, south]
    barrier = pltpu.get_barrier_semaphore()
    for other in peers:
        pl.semaphore_signal(barrier, inc=1, device_id=other, device_id_type=MESH)

    def iota(shape, axis):
        return lax.broadcasted_iota(jnp.int32, shape, axis)

    def as_f32(mask):
        return jnp.where(mask, 1.0, 0.0)

    def expert_of(column, slot, relocated, moves):
        column = column + chips * relocated * moves
        return (column - n_cols * as_f32(column >= n_cols)) * slots + slot

    top = ids_ref.shape[0]
    own_ref[:, 0:width] = own_tokens[...]
    own_ref[:, width : 2 * width] = own_upstream[...]
    gates = gates_ref[...]
    first = gates.astype(jnp.bfloat16).astype(jnp.float32)
    second = (gates - first).astype(jnp.bfloat16).astype(jnp.float32)
    third = gates - first - second
    columns = jnp.concatenate([ids_ref[...].astype(jnp.float32), first, second, third], axis=0)
    spread_out = as_f32(iota((4 * top, 128), 0) == iota((4 * top, 128), 1))
    meta = lax.dot_general(columns, spread_out, contract_first, preferred_element_type=jnp.float32)
    own_ref[:, 2 * width :] = meta.astype(jnp.bfloat16)
    moves = moves_ref[...].astype(jnp.float32)
    here = iota((slots, n_cols), 1) == e
    relocated_here = jnp.sum(jnp.where(here, moves, 0.0), axis=1, keepdims=True)
    flag = jnp.sum(
        jnp.where(iota((slots, 1), 0) == my_x, relocated_here, 0.0), axis=0, keepdims=True
    )
    served = expert_of(
        jnp.full((slots, 1), e, jnp.int32).astype(jnp.float32), iota((slots, 1), 0).astype(jnp.float32),
        relocated_here, jnp.where(early, 1.0, 0.0),
    )
    lane_ids = jnp.sum(
        jnp.where(iota((slots, 128), 1) // seats == iota((slots, 128), 0), served, 0.0), axis=0, keepdims=True
    ) - as_f32(iota((1, 128), 1) >= slots * seats)
    row_of = iota((slots * seats, 128), 0) // seats
    row_ids = sum(jnp.where(row_of == q, served[q : q + 1], 0.0) for q in range(slots))
    per_place = slots * CAP
    n_home = n_cols * per_place
    lane = iota((1, n_home), 1)
    index, rest = lane // (2 * per_place), lane // per_place % 2
    shift = jnp.where(index % 2 == 1, (index + 1) // 2, -(index // 2))
    column = 2 * lax.rem(chip + shift + chips, chips) + jnp.where(rest == 0, core, 1 - core)
    slot = lane // CAP % slots
    moved_there = jnp.dot(
        moves, as_f32(iota((n_cols, n_home), 0) == column), preferred_element_type=jnp.float32
    )
    moved_there = jnp.sum(
        jnp.where(iota((slots, n_home), 0) == slot, moved_there, 0.0), axis=0, keepdims=True
    )
    from_expert = expert_of(
        column.astype(jnp.float32), slot.astype(jnp.float32), moved_there, as_f32(moves_weights(column))
    )
    named = meta[:, 0:1] == from_expert
    for k in range(1, top):
        named = named | (meta[:, k : k + 1] == from_expert)
    before = as_f32(iota((tok_dev, tok_dev), 1) < iota((tok_dev, tok_dev), 0))
    ranks = jnp.dot(before, as_f32(named), preferred_element_type=jnp.float32)
    picks = as_f32(named & (ranks == (lane % CAP).astype(jnp.float32))).astype(jnp.bfloat16)
    pl.semaphore_wait(barrier, len(peers))
    started = []

    def go(copy):
        copy.start()
        started.append(copy)

    def landed(ref, send_sem, recv_sem, who):
        remote(ref, ref, send_sem, recv_sem, who).wait_recv()

    def spot(shift, other, h):
        index = order.index(shift) * 2 + other
        return held.at[index // per_group, pl.ds(index % per_group * tok_dev, tok_dev), cuts[h]]

    def source(shift, h):
        return own_ref.at[:, cuts[h]] if shift == 0 else spot(shift, 0, h)

    def up(hops, r, h):
        send, recv = ((send_p1, recv_p1), (send_p2, recv_p2))[hops - 1]
        return remote(source(-2 * r, h), spot(-2 * r - hops, 0, h), send.at[r, h], recv.at[r, h], ahead[hops - 1])

    def down(hops, r, h):
        send, recv = ((send_m1, recv_m1), (send_m2, recv_m2))[hops - 1]
        return remote(source(2 * r, h), spot(2 * r + hops, 0, h), send.at[r, h], recv.at[r, h], behind[hops - 1])

    def side(shift, h):
        index = order.index(shift)
        return remote(source(shift, h), spot(shift, 1, h), send_s.at[index, h], recv_s.at[index, h], twin)

    x_of = [lax.rem(my_x + k, SLICES) for k in range(SLICES)]
    y_of = [lax.rem(my_y + k, SLICES) for k in range(SLICES)]
    low, high = pl.ds(0, width), pl.ds(width, width)

    def x_copy(g, k):
        far = SLICES - k
        return remote(
            sent.at[g, x_of[k]], rows_in.at[g, my_y, my_x], send_x.at[g, far], recv_x.at[g, far], at(k, 0)
        )

    def y_send(g, k, src):
        block = rows_in.at[g, my_y, x_of[k]]
        go(remote(src, block, send_y.at[g, 0, k], recv_y.at[g, 0, k], north))
        go(remote(src, block, send_y.at[g, 1, k], recv_y.at[g, 1, k], south))

    def x_then_y(g):
        for k in (1, 3, 2):
            block = rows_in.at[g, my_y, x_of[k]]
            landed(block, send_x.at[g, k], recv_x.at[g, k], at(k, 0))
            y_send(g, k, block)

    def pass_on(g):
        for k in (0, 1, 3, 2):
            landed(rows_in.at[g, y_of[3], x_of[k]], send_y.at[g, 0, k], recv_y.at[g, 0, k], south)
            part = rows_in.at[g, y_of[3], x_of[k], :, low]
            go(remote(part, part, send_f.at[g, 0, k], recv_f.at[g, 0, k], north))
            landed(rows_in.at[g, y_of[1], x_of[k]], send_y.at[g, 1, k], recv_y.at[g, 1, k], north)
            part = rows_in.at[g, y_of[1], x_of[k], :, high]
            go(remote(part, part, send_f.at[g, 1, k], recv_f.at[g, 1, k], south))

    def finish(g):
        for k in (0, 1, 3, 2):
            landed(rows_in.at[g, y_of[2], x_of[k], :, low], send_f.at[g, 0, k], recv_f.at[g, 0, k], south)
            landed(rows_in.at[g, y_of[2], x_of[k], :, high], send_f.at[g, 1, k], recv_f.at[g, 1, k], north)

    keeps = []

    def choose(g):
        for index in range(g * per_group, (g + 1) * per_group):
            if index % 2 == 1:
                for h in range(n_cut):
                    side(order[index // 2], h).wait_recv()
        x_rows, d_rows = pick_rows(held[g], lane_ids, row_ids, tok_dev, seats)
        for q in range(slots):
            sent[g, q, :, 0:width] = x_rows[q * seats : (q + 1) * seats]
            sent[g, q, :, width : 2 * width] = d_rows[q * seats : (q + 1) * seats]
        for k in (2, 1, 3):
            go(x_copy(g, k))
        y_send(g, 0, sent.at[g, my_x])
        keep = pltpu.make_async_copy(sent.at[g, my_x], rows_in.at[g, my_y, my_x], keep_x.at[g])
        keep.start()
        keeps.append(keep)

    for hops in (2, 1):
        for h in range(n_cut):
            go(up(hops, 0, h))
            go(down(hops, 0, h))
    for h in range(n_cut):
        go(side(0, h))
    own = pltpu.make_async_copy(own_ref, held.at[0, pl.ds(0, tok_dev)], keep_sem)
    own.start()
    gate_up_at, down_at = pl.ds(0, 2 * f_slice), pl.ds(2 * f_slice, f_slice)
    loads = [
        pltpu.make_async_copy(gate_up_ref, weights.at[gate_up_at], load_w.at[0]),
        pltpu.make_async_copy(down_ref, weights.at[down_at], load_w.at[1]),
    ]
    for load in loads:
        load.start()
    own.wait()
    for r in range(1, relays + 1):
        more = r < relays
        for h in range(n_cut):
            up(2, r - 1, h).wait_recv()
            if more:
                go(up(2, r, h))
                down(2, r - 1, h).wait_recv()
                if r < relays - 1:
                    go(down(2, r, h))
        if more:
            for h in range(n_cut):
                go(up(1, r, h))
                go(down(1, r, h))
        for h in range(n_cut):
            go(side(-2 * r, h))
            if more:
                go(side(2 * r, h))
        for h in range(n_cut):
            up(1, r - 1, h).wait_recv()
            go(side(1 - 2 * r, h))
            down(1, r - 1, h).wait_recv()
            go(side(2 * r - 1, h))
        if r == relays:
            w_copies = [
                remote(gate_up_ref, far_weights.at[gate_up_at], send_w.at[0], recv_w.at[0], across),
                remote(down_ref, far_weights.at[down_at], send_w.at[1], recv_w.at[1], across),
            ]

            @pl.when(early)
            def _():
                for copy in w_copies:
                    copy.start()

        choose(r - 1)
        if r >= 2:
            x_then_y(r - 2)
        if r >= 3:
            pass_on(r - 3)
    last = groups - 1
    pass_on(last - 1)
    x_then_y(last)
    pass_on(last)
    for g in range(groups):
        finish(g)
    for keep in keeps:
        keep.wait()
    for load in loads:
        load.wait()

    @pl.when(early)
    def _():
        for copy in w_copies:
            copy.wait()
        moved = jnp.broadcast_to(flag, (f_slice, width)) > 0.5
        for i in range(3):
            at_rows = pl.ds(i * f_slice, f_slice)
            weights[at_rows] = jnp.where(
                moved, far_weights[at_rows].astype(jnp.float32), weights[at_rows].astype(jnp.float32)
            ).astype(jnp.bfloat16)

    w_gate, w_up, w_down = (pl.ds(i * f_slice, f_slice) for i in range(3))

    def x_and_d(g):
        block = rows_in[g].reshape(block_rows, 2 * width)
        return block[:, :width], block[:, width:]

    def forward(g, _):
        x, d = x_and_d(g)
        dot = functools.partial(lax.dot_general, dimension_numbers=contract_last, preferred_element_type=jnp.float32)
        up_pre = dot(x, weights[w_up])
        activated, slope_of = silu_parts(dot(x, weights[w_gate]))
        hidden_grad = dot(d, weights[w_down])
        hidden_all[g] = (activated * up_pre).astype(jnp.bfloat16)
        da_all[g] = (hidden_grad * up_pre * slope_of).astype(jnp.bfloat16)
        db_all[g] = (hidden_grad * activated).astype(jnp.bfloat16)
        return 0

    lax.fori_loop(0, groups, forward, 0)
    every_row = rows_in[...].reshape(groups * block_rows, 2 * width)
    g_copies, g_places = [], []
    for i, (left, lo) in enumerate(((da_all, 0), (db_all, 0), (hidden_all, width))):
        at_rows = pl.ds(i * f_slice, f_slice)
        out_ref, out_rows = ((grad_gate_up_ref, at_rows), (grad_down_ref, pl.ds(0, f_slice)))[i // 2]
        out_ref[out_rows] = lax.dot_general(
            left[...].reshape(groups * block_rows, f_slice), every_row[:, lo : lo + width], contract_first,
            preferred_element_type=jnp.float32,
        ).astype(jnp.bfloat16)
        g_places.append((out_ref, out_rows, at_rows))
        g_copies.append(
            remote(out_ref.at[out_rows], far_grads.at[at_rows], send_g.at[i], recv_g.at[i], across)
        )

    @pl.when(jnp.logical_not(early))
    def _():
        for copy in g_copies:
            copy.start()

    pair = SLICES // 2

    def relay_copy(g, way, i):
        block = pair * (1 - way) + i
        return remote(
            part_ref.at[g, y_of[2], block], relay.at[g, way, i], send_r.at[g, way, i], recv_r.at[g, way, i],
            (north, south)[way],
        )

    def direct_copy(g, way, i):
        block = pair * way + i
        return remote(
            part_ref.at[g, y_of[1 if way == 0 else 3], block], got.at[g, way, block],
            send_d.at[g, way, i], recv_d.at[g, way, i], (north, south)[way],
        )

    def total_copy(g, way, i):
        block = pair * (1 - way) + i
        return remote(
            summed.at[g, way, i], got.at[g, way, block], send_t.at[g, way, i], recv_t.at[g, way, i],
            (north, south)[way],
        )

    every = [(way, i) for i in range(pair) for way in range(2)]
    for g in range(groups):
        part = jnp.dot(
            da_all[g], weights[w_gate], preferred_element_type=jnp.float32
        ) + jnp.dot(db_all[g], weights[w_up], preferred_element_type=jnp.float32)
        part_ref[g] = part.astype(jnp.bfloat16).reshape(SLICES, slots, seats, width)
        for way, i in every:
            go(relay_copy(g, way, i))
        for way, i in every:
            go(direct_copy(g, way, i))
    for g in range(groups):
        for way, i in every:
            relay_copy(g, way, i).wait_recv()
            mine = part_ref[g, y_of[1 if way == 0 else 3], pair * (1 - way) + i].astype(jnp.float32)
            summed[g, way, i] = (mine + relay[g, way, i].astype(jnp.float32)).astype(jnp.bfloat16)
            go(total_copy(g, way, i))
    back_keeps = []

    n_rows = slots * seats
    to_row = lax.broadcasted_iota(jnp.int32, (n_rows, n_rows), 0)
    from_row = lax.broadcasted_iota(jnp.int32, (n_rows, n_rows), 1)
    wanted = (to_row % per_place) // CAP * seats + to_row // per_place * CAP + to_row % CAP
    regroup = jnp.where(from_row == wanted, 1.0, 0.0).astype(jnp.bfloat16)

    def send_home(g):
        for k in (1, 3, 2):
            landed(back.at[g, x_of[k]], send_b.at[g, k], recv_b.at[g, k], at(k, 0))
        back_keeps[g].wait()
        rows = jnp.dot(
            regroup, back[g].reshape(n_rows, width), preferred_element_type=jnp.float32
        ).astype(jnp.bfloat16)
        places[pl.ds(g * per_group, per_group)] = rows.reshape(per_group, per_place, width)
        for place in reversed(range(g * per_group, (g + 1) * per_group)):
            if place > 0:
                go(remote(
                    places.at[place], home.at[seen(place)], send_h.at[seen(place)], recv_h.at[seen(place)], peer(place)
                ))

    for g in range(groups):
        for way, i in every:
            direct_copy(g, way, i).wait_recv()
            total_copy(g, way, i).wait_recv()
        for k in (2, 1, 3, 0):
            block = x_of[k]
            total[g, block] = (
                part_ref[g, my_y, block].astype(jnp.float32)
                + got[g, 0, block].astype(jnp.float32)
                + got[g, 1, block].astype(jnp.float32)
            ).astype(jnp.bfloat16)
            if k > 0:
                far = SLICES - k
                go(remote(
                    total.at[g, block], back.at[g, my_x], send_b.at[g, far], recv_b.at[g, far], at(k, 0)
                ))
            else:
                keep = pltpu.make_async_copy(total.at[g, block], back.at[g, my_x], keep_b.at[g])
                keep.start()
                back_keeps.append(keep)
        if g > 0:
            send_home(g - 1)
    send_home(groups - 1)
    keep = pltpu.make_async_copy(places.at[0], home.at[0], keep_h)
    keep.start()
    keep.wait()
    for place in range(1, n_cols):
        landed(home.at[place], send_h.at[place], recv_h.at[place], peer(place))
    tokens_ref[...] = jnp.dot(
        picks, home[...].reshape(n_cols * per_place, width), preferred_element_type=jnp.float32
    ).astype(tokens_ref.dtype)

    @pl.when(jnp.logical_not(early))
    def _():
        for copy in g_copies:
            copy.wait()
        came = jnp.broadcast_to(flag, (f_slice, width)) > 0.5
        for out_ref, out_rows, at_rows in g_places:
            out_ref[out_rows] = jnp.where(
                came, far_grads[at_rows].astype(jnp.float32), out_ref[out_rows].astype(jnp.float32)
            ).astype(jnp.bfloat16)

    for copy in started:
        copy.wait_send()


def whole_step(tokens, upstream, ids, gates, moves, gate_up, down):
    tok_dev, width = tokens.shape
    slots, n_cols = moves.shape
    full = 2 * width + 128
    chips = n_cols // 2
    groups = 4
    seats = n_cols * CAP // groups
    f_slice = down.shape[0]
    block_rows = SLICES * slots * seats
    pair = SLICES // 2
    relays = chips // 4
    cut = 2
    bf16 = jnp.bfloat16
    dma = pltpu.SemaphoreType.DMA
    any_spec = pl.BlockSpec(memory_space=pl.ANY)
    return pl.pallas_call(
        functools.partial(step_kernel, n_cols),
        out_shape=tuple(
            jax.ShapeDtypeStruct((rows, width), bf16) for rows in (tok_dev, 2 * f_slice, f_slice)
        ),
        in_specs=[VMEM_SPEC] * 5 + [any_spec] * 2,
        out_specs=(VMEM_SPEC,) * 3,
        scratch_shapes=[
            pltpu.VMEM((tok_dev, full), bf16),
            pltpu.VMEM((3 * f_slice, width), bf16),
            pltpu.VMEM((groups, n_cols // groups * tok_dev, full), bf16),
            pltpu.VMEM((groups, slots, seats, 2 * width), bf16),
            pltpu.VMEM((groups, SLICES, slots, seats, 2 * width), bf16),
            pltpu.VMEM((3 * f_slice, width), bf16),
            pltpu.VMEM((3 * f_slice, width), bf16),
            pltpu.VMEM((groups, block_rows, f_slice), bf16),
            pltpu.VMEM((groups, block_rows, f_slice), bf16),
            pltpu.VMEM((groups, block_rows, f_slice), bf16),
            pltpu.VMEM((groups, SLICES, slots, seats, width), bf16),
            pltpu.VMEM((groups, 2, pair, seats, width), bf16),
            pltpu.VMEM((groups, 2, pair, seats, width), bf16),
            pltpu.VMEM((groups, 2, slots, seats, width), bf16),
            pltpu.VMEM((groups, slots, seats, width), bf16),
            pltpu.VMEM((groups, slots, seats, width), bf16),
            pltpu.VMEM((n_cols, slots * CAP, width), bf16),
            pltpu.VMEM((n_cols, slots * CAP, width), bf16),
            dma,
        ] + [dma((relays, cut))] * 8 + [
            dma((chips, cut)), dma((chips, cut)),
            dma((groups,)), dma((groups, SLICES)), dma((groups, SLICES)),
            dma((groups, 2, SLICES)), dma((groups, 2, SLICES)),
            dma((groups, 2, SLICES)), dma((groups, 2, SLICES)),
            dma((2,)), dma((2,)), dma((2,)), dma((3,)), dma((3,)),
        ] + [dma((groups, 2, pair))] * 6 + [
            dma((groups, SLICES)), dma((groups, SLICES)), dma((groups,)),
            dma((n_cols,)), dma((n_cols,)), dma,
        ],
        compiler_params=pltpu.CompilerParams(
            collective_id=0, has_side_effects=True, vmem_limit_bytes=56 * 1024 * 1024
        ),
        name="whole_step",
    )(tokens, upstream, ids, gates, moves, gate_up, down)


def per_device(tokens, upstream, expert_ids, gates, relocate, w_gate_up, w_down):
    grad_tokens, grad_gate_up, grad_down = whole_step(
        tokens, upstream, expert_ids.T, gates.T, relocate.T, w_gate_up[0, 0], w_down[0, 0]
    )
    return (grad_tokens, grad_gate_up.reshape(w_gate_up.shape), grad_down.reshape(w_down.shape))


def solution(mesh):
    return jax.shard_map(
        per_device,
        mesh=mesh,
        in_specs=(
            P(("dp", "expert"), None),
            P(("dp", "expert"), None),
            P(("dp", "expert"), None),
            P(("dp", "expert"), None),
            P(),
            P("expert", "dp", None, None),
            P("expert", "dp", None, None),
        ),
        out_specs=(
            P(("dp", "expert"), None),
            P("expert", "dp", None, None),
            P("expert", "dp", None, None),
        ),
        check_vma=False,
    )
```

```python
import functools

import jax
import jax.numpy as jnp
from jax import lax
from jax.experimental import pallas as pl
from jax.experimental.pallas import tpu as pltpu
from jax.sharding import PartitionSpec as P

SLICES = 4
CAP = 2
MESH = pl.DeviceIdType.MESH

contract_last = (((1,), (1,)), ((), ()))
contract_first = (((0,), (0,)), ((), ()))
VMEM_SPEC = pl.BlockSpec(memory_space=pltpu.VMEM)


def silu_parts(values_in):
    sigmoid_of = jax.nn.sigmoid(values_in)
    return (values_in * sigmoid_of, sigmoid_of * (1.0 + values_in * (1.0 - sigmoid_of)))


def remote(src, dst, send_sem, recv_sem, peer):
    return pltpu.make_async_remote_copy(
        src_ref=src, dst_ref=dst, send_sem=send_sem, recv_sem=recv_sem,
        device_id=peer, device_id_type=MESH,
    )


def xy_peers():
    row = lax.axis_index("dp")
    my_x, my_y = row // SLICES, lax.rem(row, SLICES)

    def at(dx, dy):
        return {"dp": lax.rem(my_x + dx, SLICES) * SLICES + lax.rem(my_y + dy, SLICES)}

    return my_x, my_y, at


def near_order(chips):
    order = [0]
    for s in range(1, chips // 2):
        order += [s, -s]
    return order + [-(chips // 2)]


def pick_rows(block, lane_ids, row_ids, tok_dev, seats):
    n_tok, width = block.shape[0], (block.shape[1] - 128) // 2
    top = 8
    meta = block[:, 2 * width :].astype(jnp.float32)
    hit = meta[:, 0:1] == lane_ids
    for k in range(1, top):
        hit = hit | (meta[:, k : k + 1] == lane_ids)
    hits = jnp.where(hit, 1.0, 0.0)
    t_row = lax.broadcasted_iota(jnp.int32, (n_tok, n_tok), 0)
    t_col = lax.broadcasted_iota(jnp.int32, (n_tok, n_tok), 1)
    earlier = (t_row // tok_dev == t_col // tok_dev) & (t_col < t_row)
    ranks = jnp.dot(
        jnp.where(earlier, 1.0, 0.0).astype(jnp.bfloat16), hits.astype(jnp.bfloat16),
        preferred_element_type=jnp.float32,
    )
    device = (lax.broadcasted_iota(jnp.int32, hits.shape, 0) // tok_dev).astype(jnp.float32)
    seat = lax.rem(lax.broadcasted_iota(jnp.int32, hits.shape, 1), seats).astype(jnp.float32)
    chosen = hit & (CAP * device + ranks == seat)
    one_hot = jnp.where(chosen, 1.0, 0.0).astype(jnp.bfloat16)
    rows = lax.dot_general(one_hot, block, contract_first, preferred_element_type=jnp.float32)
    rows = rows[: row_ids.shape[0]]
    meta_rows = rows[:, 2 * width :]
    gates = sum(pltpu.roll(meta_rows, 128 - top * part, 1) for part in (1, 2, 3))
    lane = lax.broadcasted_iota(jnp.int32, meta_rows.shape, 1)
    gate = jnp.sum(
        jnp.where((lane < top) & (meta_rows == row_ids), gates, 0.0), axis=1, keepdims=True
    )
    return rows[:, :width].astype(jnp.bfloat16), (gate * rows[:, width : 2 * width]).astype(jnp.bfloat16)


def moves_weights(e):
    return (lax.rem(e, 2) == 0) & (lax.rem(e // 2, 8) < 6)


def step_kernel(
    n_cols, own_tokens, own_upstream, ids_ref, gates_ref, moves_ref, gate_up_ref, down_ref,
    tokens_ref, grad_gate_up_ref, grad_down_ref,
    own_ref, far_grads, held, sent, rows_in, weights, far_weights, da_all, db_all, hidden_all,
    part_ref, relay, summed, got, total, back, places, home,
    keep_sem, send_p2, recv_p2, send_p1, recv_p1, send_m2, recv_m2, send_m1, recv_m1, send_s, recv_s,
    keep_x, send_x, recv_x, send_y, recv_y, send_f, recv_f,
    load_w, send_w, recv_w, send_g, recv_g,
    send_r, recv_r, send_d, recv_d, send_t, recv_t, send_b, recv_b, keep_b,
    send_h, recv_h, keep_h,
):
    e = lax.axis_index("expert")
    chips = n_cols // 2
    order = near_order(chips)
    chip, core = e // 2, lax.rem(e, 2)
    my_x, my_y, at = xy_peers()
    north, south = at(0, 1), at(0, 3)
    ahead, behind = [
        [{"expert": lax.rem(e + sign * 2 * hops + n_cols, n_cols)} for hops in (1, 2)] for sign in (1, -1)
    ]
    twin = {"expert": e + 1 - 2 * core}
    across = {"expert": lax.rem(e + chips, n_cols)}
    tok_dev, full = own_ref.shape
    width = (full - 128) // 2
    groups, slots = sent.shape[0], sent.shape[1]
    seats = sent.shape[2]
    block_rows = SLICES * slots * seats
    per_group = seats // CAP
    f_slice = down_ref.shape[0]
    cuts = [pl.ds(0, width), pl.ds(width, width + 128)]
    n_cut = len(cuts)
    relays = chips // 4
    early = moves_weights(e)

    def peer(place):
        z = lax.rem(chip + order[place // 2] + chips, chips)
        return {"expert": 2 * z + (core if place % 2 == 0 else 1 - core)}

    def seen(place):
        shift = -order[place // 2]
        return order.index(shift if shift < chips // 2 else -shift) * 2 + place % 2

    peers = [peer(place) for place in range(1, n_cols)] + [at(1, 0), at(2, 0), at(3, 0), north, south]
    barrier = pltpu.get_barrier_semaphore()
    for other in peers:
        pl.semaphore_signal(barrier, inc=1, device_id=other, device_id_type=MESH)

    def iota(shape, axis):
        return lax.broadcasted_iota(jnp.int32, shape, axis)

    def as_f32(mask):
        return jnp.where(mask, 1.0, 0.0)

    def expert_of(column, slot, relocated, moves):
        column = column + chips * relocated * moves
        return (column - n_cols * as_f32(column >= n_cols)) * slots + slot

    top = ids_ref.shape[0]
    own_ref[:, 0:width] = own_tokens[...]
    own_ref[:, width : 2 * width] = own_upstream[...]
    gates = gates_ref[...]
    first = gates.astype(jnp.bfloat16).astype(jnp.float32)
    second = (gates - first).astype(jnp.bfloat16).astype(jnp.float32)
    third = gates - first - second
    columns = jnp.concatenate([ids_ref[...].astype(jnp.float32), first, second, third], axis=0)
    spread_out = as_f32(iota((4 * top, 128), 0) == iota((4 * top, 128), 1))
    meta = lax.dot_general(columns, spread_out, contract_first, preferred_element_type=jnp.float32)
    own_ref[:, 2 * width :] = meta.astype(jnp.bfloat16)
    moves = moves_ref[...].astype(jnp.float32)
    here = iota((slots, n_cols), 1) == e
    relocated_here = jnp.sum(jnp.where(here, moves, 0.0), axis=1, keepdims=True)
    flag = jnp.sum(
        jnp.where(iota((slots, 1), 0) == my_x, relocated_here, 0.0), axis=0, keepdims=True
    )
    served = expert_of(
        jnp.full((slots, 1), e, jnp.int32).astype(jnp.float32), iota((slots, 1), 0).astype(jnp.float32),
        relocated_here, jnp.where(early, 1.0, 0.0),
    )
    lane_ids = jnp.sum(
        jnp.where(iota((slots, 128), 1) // seats == iota((slots, 128), 0), served, 0.0), axis=0, keepdims=True
    ) - as_f32(iota((1, 128), 1) >= slots * seats)
    row_of = iota((slots * seats, 128), 0) // seats
    row_ids = sum(jnp.where(row_of == q, served[q : q + 1], 0.0) for q in range(slots))
    per_place = slots * CAP
    n_home = n_cols * per_place
    lane = iota((1, n_home), 1)
    index, rest = lane // (2 * per_place), lane // per_place % 2
    shift = jnp.where(index % 2 == 1, (index + 1) // 2, -(index // 2))
    column = 2 * lax.rem(chip + shift + chips, chips) + jnp.where(rest == 0, core, 1 - core)
    slot = lane // CAP % slots
    moved_there = jnp.dot(
        moves, as_f32(iota((n_cols, n_home), 0) == column), preferred_element_type=jnp.float32
    )
    moved_there = jnp.sum(
        jnp.where(iota((slots, n_home), 0) == slot, moved_there, 0.0), axis=0, keepdims=True
    )
    from_expert = expert_of(
        column.astype(jnp.float32), slot.astype(jnp.float32), moved_there, as_f32(moves_weights(column))
    )
    named = meta[:, 0:1] == from_expert
    for k in range(1, top):
        named = named | (meta[:, k : k + 1] == from_expert)
    before = as_f32(iota((tok_dev, tok_dev), 1) < iota((tok_dev, tok_dev), 0))
    ranks = jnp.dot(before, as_f32(named), preferred_element_type=jnp.float32)
    picks = as_f32(named & (ranks == (lane % CAP).astype(jnp.float32))).astype(jnp.bfloat16)
    pl.semaphore_wait(barrier, len(peers))
    started = []

    def go(copy):
        copy.start()
        started.append(copy)

    def landed(ref, send_sem, recv_sem, who):
        remote(ref, ref, send_sem, recv_sem, who).wait_recv()

    def spot(shift, other, h):
        index = order.index(shift) * 2 + other
        return held.at[index // per_group, pl.ds(index % per_group * tok_dev, tok_dev), cuts[h]]

    def source(shift, h):
        return own_ref.at[:, cuts[h]] if shift == 0 else spot(shift, 0, h)

    def up(hops, r, h):
        send, recv = ((send_p1, recv_p1), (send_p2, recv_p2))[hops - 1]
        return remote(source(-2 * r, h), spot(-2 * r - hops, 0, h), send.at[r, h], recv.at[r, h], ahead[hops - 1])

    def down(hops, r, h):
        send, recv = ((send_m1, recv_m1), (send_m2, recv_m2))[hops - 1]
        return remote(source(2 * r, h), spot(2 * r + hops, 0, h), send.at[r, h], recv.at[r, h], behind[hops - 1])

    def side(shift, h):
        index = order.index(shift)
        return remote(source(shift, h), spot(shift, 1, h), send_s.at[index, h], recv_s.at[index, h], twin)

    x_of = [lax.rem(my_x + k, SLICES) for k in range(SLICES)]
    y_of = [lax.rem(my_y + k, SLICES) for k in range(SLICES)]
    low, high = pl.ds(0, width), pl.ds(width, width)

    def x_copy(g, k):
        far = SLICES - k
        return remote(
            sent.at[g, x_of[k]], rows_in.at[g, my_y, my_x], send_x.at[g, far], recv_x.at[g, far], at(k, 0)
        )

    def y_send(g, k, src):
        block = rows_in.at[g, my_y, x_of[k]]
        go(remote(src, block, send_y.at[g, 0, k], recv_y.at[g, 0, k], north))
        go(remote(src, block, send_y.at[g, 1, k], recv_y.at[g, 1, k], south))

    def x_then_y(g):
        for k in (1, 3, 2):
            block = rows_in.at[g, my_y, x_of[k]]
            landed(block, send_x.at[g, k], recv_x.at[g, k], at(k, 0))
            y_send(g, k, block)

    def pass_on(g):
        for k in (0, 1, 3, 2):
            landed(rows_in.at[g, y_of[3], x_of[k]], send_y.at[g, 0, k], recv_y.at[g, 0, k], south)
            part = rows_in.at[g, y_of[3], x_of[k], :, low]
            go(remote(part, part, send_f.at[g, 0, k], recv_f.at[g, 0, k], north))
            landed(rows_in.at[g, y_of[1], x_of[k]], send_y.at[g, 1, k], recv_y.at[g, 1, k], north)
            part = rows_in.at[g, y_of[1], x_of[k], :, high]
            go(remote(part, part, send_f.at[g, 1, k], recv_f.at[g, 1, k], south))

    def finish(g):
        for k in (0, 1, 3, 2):
            landed(rows_in.at[g, y_of[2], x_of[k], :, low], send_f.at[g, 0, k], recv_f.at[g, 0, k], south)
            landed(rows_in.at[g, y_of[2], x_of[k], :, high], send_f.at[g, 1, k], recv_f.at[g, 1, k], north)

    keeps = []

    def choose(g):
        for index in range(g * per_group, (g + 1) * per_group):
            if index % 2 == 1:
                for h in range(n_cut):
                    side(order[index // 2], h).wait_recv()
        x_rows, d_rows = pick_rows(held[g], lane_ids, row_ids, tok_dev, seats)
        for q in range(slots):
            sent[g, q, :, 0:width] = x_rows[q * seats : (q + 1) * seats]
            sent[g, q, :, width : 2 * width] = d_rows[q * seats : (q + 1) * seats]
        for k in (2, 1, 3):
            go(x_copy(g, k))
        y_send(g, 0, sent.at[g, my_x])
        keep = pltpu.make_async_copy(sent.at[g, my_x], rows_in.at[g, my_y, my_x], keep_x.at[g])
        keep.start()
        keeps.append(keep)

    for hops in (2, 1):
        for h in range(n_cut):
            go(up(hops, 0, h))
            go(down(hops, 0, h))
    for h in range(n_cut):
        go(side(0, h))
    own = pltpu.make_async_copy(own_ref, held.at[0, pl.ds(0, tok_dev)], keep_sem)
    own.start()
    gate_up_at, down_at = pl.ds(0, 2 * f_slice), pl.ds(2 * f_slice, f_slice)
    loads = [
        pltpu.make_async_copy(gate_up_ref, weights.at[gate_up_at], load_w.at[0]),
        pltpu.make_async_copy(down_ref, weights.at[down_at], load_w.at[1]),
    ]
    for load in loads:
        load.start()
    own.wait()
    for r in range(1, relays + 1):
        more = r < relays
        for h in range(n_cut):
            up(2, r - 1, h).wait_recv()
            if more:
                go(up(2, r, h))
                down(2, r - 1, h).wait_recv()
                if r < relays - 1:
                    go(down(2, r, h))
        if more:
            for h in range(n_cut):
                go(up(1, r, h))
                go(down(1, r, h))
        for h in range(n_cut):
            go(side(-2 * r, h))
            if more:
                go(side(2 * r, h))
        for h in range(n_cut):
            up(1, r - 1, h).wait_recv()
            go(side(1 - 2 * r, h))
            down(1, r - 1, h).wait_recv()
            go(side(2 * r - 1, h))
        if r == relays:
            w_copies = [
                remote(gate_up_ref, far_weights.at[gate_up_at], send_w.at[0], recv_w.at[0], across),
                remote(down_ref, far_weights.at[down_at], send_w.at[1], recv_w.at[1], across),
            ]

            @pl.when(early)
            def _():
                for copy in w_copies:
                    copy.start()

        choose(r - 1)
        if r >= 2:
            x_then_y(r - 2)
        if r >= 3:
            pass_on(r - 3)
    last = groups - 1
    pass_on(last - 1)
    x_then_y(last)
    pass_on(last)
    for g in range(groups):
        finish(g)
    for keep in keeps:
        keep.wait()
    for load in loads:
        load.wait()

    @pl.when(early)
    def _():
        for copy in w_copies:
            copy.wait()
        moved = jnp.broadcast_to(flag, (f_slice, width)) > 0.5
        for i in range(3):
            at_rows = pl.ds(i * f_slice, f_slice)
            weights[at_rows] = jnp.where(
                moved, far_weights[at_rows].astype(jnp.float32), weights[at_rows].astype(jnp.float32)
            ).astype(jnp.bfloat16)

    w_gate, w_up, w_down = (pl.ds(i * f_slice, f_slice) for i in range(3))

    def x_and_d(g):
        block = rows_in[g].reshape(block_rows, 2 * width)
        return block[:, :width], block[:, width:]

    def forward(g, _):
        x, d = x_and_d(g)
        dot = functools.partial(lax.dot_general, dimension_numbers=contract_last, preferred_element_type=jnp.float32)
        up_pre = dot(x, weights[w_up])
        activated, slope_of = silu_parts(dot(x, weights[w_gate]))
        hidden_grad = dot(d, weights[w_down])
        hidden_all[g] = (activated * up_pre).astype(jnp.bfloat16)
        da_all[g] = (hidden_grad * up_pre * slope_of).astype(jnp.bfloat16)
        db_all[g] = (hidden_grad * activated).astype(jnp.bfloat16)
        return 0

    lax.fori_loop(0, groups, forward, 0)
    every_row = rows_in[...].reshape(groups * block_rows, 2 * width)
    g_copies, g_places = [], []
    for i, (left, lo) in enumerate(((da_all, 0), (db_all, 0), (hidden_all, width))):
        at_rows = pl.ds(i * f_slice, f_slice)
        out_ref, out_rows = ((grad_gate_up_ref, at_rows), (grad_down_ref, pl.ds(0, f_slice)))[i // 2]
        out_ref[out_rows] = lax.dot_general(
            left[...].reshape(groups * block_rows, f_slice), every_row[:, lo : lo + width], contract_first,
            preferred_element_type=jnp.float32,
        ).astype(jnp.bfloat16)
        g_places.append((out_ref, out_rows, at_rows))
        g_copies.append(
            remote(out_ref.at[out_rows], far_grads.at[at_rows], send_g.at[i], recv_g.at[i], across)
        )

        @pl.when(jnp.logical_not(early))
        def _(copy=g_copies[-1]):
            copy.start()

    pair = SLICES // 2

    def relay_copy(g, way, i):
        block = pair * (1 - way) + i
        return remote(
            part_ref.at[g, y_of[2], block], relay.at[g, way, i], send_r.at[g, way, i], recv_r.at[g, way, i],
            (north, south)[way],
        )

    def direct_copy(g, way, i):
        block = pair * way + i
        return remote(
            part_ref.at[g, y_of[1 if way == 0 else 3], block], got.at[g, way, block],
            send_d.at[g, way, i], recv_d.at[g, way, i], (north, south)[way],
        )

    def total_copy(g, way, i):
        block = pair * (1 - way) + i
        return remote(
            summed.at[g, way, i], got.at[g, way, block], send_t.at[g, way, i], recv_t.at[g, way, i],
            (north, south)[way],
        )

    every = [(way, i) for i in range(pair) for way in range(2)]
    for g in range(groups):
        part = jnp.dot(
            da_all[g], weights[w_gate], preferred_element_type=jnp.float32
        ) + jnp.dot(db_all[g], weights[w_up], preferred_element_type=jnp.float32)
        part_ref[g] = part.astype(jnp.bfloat16).reshape(SLICES, slots, seats, width)
        for way, i in every:
            go(relay_copy(g, way, i))
        for way, i in every:
            go(direct_copy(g, way, i))
    for g in range(groups):
        for way, i in every:
            relay_copy(g, way, i).wait_recv()
            mine = part_ref[g, y_of[1 if way == 0 else 3], pair * (1 - way) + i].astype(jnp.float32)
            summed[g, way, i] = (mine + relay[g, way, i].astype(jnp.float32)).astype(jnp.bfloat16)
            go(total_copy(g, way, i))
    back_keeps = []

    n_rows = slots * seats
    to_row = lax.broadcasted_iota(jnp.int32, (n_rows, n_rows), 0)
    from_row = lax.broadcasted_iota(jnp.int32, (n_rows, n_rows), 1)
    wanted = (to_row % per_place) // CAP * seats + to_row // per_place * CAP + to_row % CAP
    regroup = jnp.where(from_row == wanted, 1.0, 0.0).astype(jnp.bfloat16)

    def send_home(g):
        for k in (1, 3, 2):
            landed(back.at[g, x_of[k]], send_b.at[g, k], recv_b.at[g, k], at(k, 0))
        back_keeps[g].wait()
        rows = jnp.dot(
            regroup, back[g].reshape(n_rows, width), preferred_element_type=jnp.float32
        ).astype(jnp.bfloat16)
        places[pl.ds(g * per_group, per_group)] = rows.reshape(per_group, per_place, width)
        for place in reversed(range(g * per_group, (g + 1) * per_group)):
            if place > 0:
                go(remote(
                    places.at[place], home.at[seen(place)], send_h.at[seen(place)], recv_h.at[seen(place)], peer(place)
                ))

    for g in range(groups):
        for way, i in every:
            direct_copy(g, way, i).wait_recv()
            total_copy(g, way, i).wait_recv()
        for k in (2, 1, 3, 0):
            block = x_of[k]
            total[g, block] = (
                part_ref[g, my_y, block].astype(jnp.float32)
                + got[g, 0, block].astype(jnp.float32)
                + got[g, 1, block].astype(jnp.float32)
            ).astype(jnp.bfloat16)
            if k > 0:
                far = SLICES - k
                go(remote(
                    total.at[g, block], back.at[g, my_x], send_b.at[g, far], recv_b.at[g, far], at(k, 0)
                ))
            else:
                keep = pltpu.make_async_copy(total.at[g, block], back.at[g, my_x], keep_b.at[g])
                keep.start()
                back_keeps.append(keep)
        if g > 0:
            send_home(g - 1)
    send_home(groups - 1)
    keep = pltpu.make_async_copy(places.at[0], home.at[0], keep_h)
    keep.start()
    keep.wait()
    for place in range(1, n_cols):
        landed(home.at[place], send_h.at[place], recv_h.at[place], peer(place))
    tokens_ref[...] = jnp.dot(
        picks, home[...].reshape(n_cols * per_place, width), preferred_element_type=jnp.float32
    ).astype(tokens_ref.dtype)

    @pl.when(jnp.logical_not(early))
    def _():
        for copy in g_copies:
            copy.wait()
        came = jnp.broadcast_to(flag, (f_slice, width)) > 0.5
        for out_ref, out_rows, at_rows in g_places:
            out_ref[out_rows] = jnp.where(
                came, far_grads[at_rows].astype(jnp.float32), out_ref[out_rows].astype(jnp.float32)
            ).astype(jnp.bfloat16)

    for copy in started:
        copy.wait_send()


def whole_step(tokens, upstream, ids, gates, moves, gate_up, down):
    tok_dev, width = tokens.shape
    slots, n_cols = moves.shape
    full = 2 * width + 128
    chips = n_cols // 2
    groups = 4
    seats = n_cols * CAP // groups
    f_slice = down.shape[0]
    block_rows = SLICES * slots * seats
    pair = SLICES // 2
    relays = chips // 4
    cut = 2
    bf16 = jnp.bfloat16
    dma = pltpu.SemaphoreType.DMA
    any_spec = pl.BlockSpec(memory_space=pl.ANY)
    return pl.pallas_call(
        functools.partial(step_kernel, n_cols),
        out_shape=tuple(
            jax.ShapeDtypeStruct((rows, width), bf16) for rows in (tok_dev, 2 * f_slice, f_slice)
        ),
        in_specs=[VMEM_SPEC] * 5 + [any_spec] * 2,
        out_specs=(VMEM_SPEC,) * 3,
        scratch_shapes=[
            pltpu.VMEM((tok_dev, full), bf16),
            pltpu.VMEM((3 * f_slice, width), bf16),
            pltpu.VMEM((groups, n_cols // groups * tok_dev, full), bf16),
            pltpu.VMEM((groups, slots, seats, 2 * width), bf16),
            pltpu.VMEM((groups, SLICES, slots, seats, 2 * width), bf16),
            pltpu.VMEM((3 * f_slice, width), bf16),
            pltpu.VMEM((3 * f_slice, width), bf16),
            pltpu.VMEM((groups, block_rows, f_slice), bf16),
            pltpu.VMEM((groups, block_rows, f_slice), bf16),
            pltpu.VMEM((groups, block_rows, f_slice), bf16),
            pltpu.VMEM((groups, SLICES, slots, seats, width), bf16),
            pltpu.VMEM((groups, 2, pair, seats, width), bf16),
            pltpu.VMEM((groups, 2, pair, seats, width), bf16),
            pltpu.VMEM((groups, 2, slots, seats, width), bf16),
            pltpu.VMEM((groups, slots, seats, width), bf16),
            pltpu.VMEM((groups, slots, seats, width), bf16),
            pltpu.VMEM((n_cols, slots * CAP, width), bf16),
            pltpu.VMEM((n_cols, slots * CAP, width), bf16),
            dma,
        ] + [dma((relays, cut))] * 8 + [
            dma((chips, cut)), dma((chips, cut)),
            dma((groups,)), dma((groups, SLICES)), dma((groups, SLICES)),
            dma((groups, 2, SLICES)), dma((groups, 2, SLICES)),
            dma((groups, 2, SLICES)), dma((groups, 2, SLICES)),
            dma((2,)), dma((2,)), dma((2,)), dma((3,)), dma((3,)),
        ] + [dma((groups, 2, pair))] * 6 + [
            dma((groups, SLICES)), dma((groups, SLICES)), dma((groups,)),
            dma((n_cols,)), dma((n_cols,)), dma,
        ],
        compiler_params=pltpu.CompilerParams(
            collective_id=0, has_side_effects=True, vmem_limit_bytes=56 * 1024 * 1024
        ),
        name="whole_step",
    )(tokens, upstream, ids, gates, moves, gate_up, down)


def per_device(tokens, upstream, expert_ids, gates, relocate, w_gate_up, w_down):
    grad_tokens, grad_gate_up, grad_down = whole_step(
        tokens, upstream, expert_ids.T, gates.T, relocate.T, w_gate_up[0, 0], w_down[0, 0]
    )
    return (grad_tokens, grad_gate_up.reshape(w_gate_up.shape), grad_down.reshape(w_down.shape))


def solution(mesh):
    return jax.shard_map(
        per_device,
        mesh=mesh,
        in_specs=(
            P(("dp", "expert"), None),
            P(("dp", "expert"), None),
            P(("dp", "expert"), None),
            P(("dp", "expert"), None),
            P(),
            P("expert", "dp", None, None),
            P("expert", "dp", None, None),
        ),
        out_specs=(
            P(("dp", "expert"), None),
            P("expert", "dp", None, None),
            P("expert", "dp", None, None),
        ),
        check_vma=False,
    )
```

```python
import functools

import jax
import jax.numpy as jnp
from jax import lax
from jax.experimental import pallas as pl
from jax.experimental.pallas import tpu as pltpu
from jax.sharding import PartitionSpec as P

SLICES = 4
CAP = 2
MESH = pl.DeviceIdType.MESH

contract_last = (((1,), (1,)), ((), ()))
contract_first = (((0,), (0,)), ((), ()))
VMEM_SPEC = pl.BlockSpec(memory_space=pltpu.VMEM)


def silu_parts(values_in):
    sigmoid_of = jax.nn.sigmoid(values_in)
    return (values_in * sigmoid_of, sigmoid_of * (1.0 + values_in * (1.0 - sigmoid_of)))


def remote(src, dst, send_sem, recv_sem, peer):
    return pltpu.make_async_remote_copy(
        src_ref=src, dst_ref=dst, send_sem=send_sem, recv_sem=recv_sem,
        device_id=peer, device_id_type=MESH,
    )


def xy_peers():
    row = lax.axis_index("dp")
    my_x, my_y = row // SLICES, lax.rem(row, SLICES)

    def at(dx, dy):
        return {"dp": lax.rem(my_x + dx, SLICES) * SLICES + lax.rem(my_y + dy, SLICES)}

    return my_x, my_y, at


def near_order(chips):
    order = [0]
    for s in range(1, chips // 2):
        order += [s, -s]
    return order + [-(chips // 2)]


def pick_rows(block, lane_ids, row_ids, tok_dev, seats):
    n_tok, width = block.shape[0], (block.shape[1] - 128) // 2
    top = 8
    meta = block[:, 2 * width :].astype(jnp.float32)
    hit = meta[:, 0:1] == lane_ids
    for k in range(1, top):
        hit = hit | (meta[:, k : k + 1] == lane_ids)
    hits = jnp.where(hit, 1.0, 0.0)
    t_row = lax.broadcasted_iota(jnp.int32, (n_tok, n_tok), 0)
    t_col = lax.broadcasted_iota(jnp.int32, (n_tok, n_tok), 1)
    earlier = (t_row // tok_dev == t_col // tok_dev) & (t_col < t_row)
    ranks = jnp.dot(
        jnp.where(earlier, 1.0, 0.0).astype(jnp.bfloat16), hits.astype(jnp.bfloat16),
        preferred_element_type=jnp.float32,
    )
    device = (lax.broadcasted_iota(jnp.int32, hits.shape, 0) // tok_dev).astype(jnp.float32)
    seat = lax.rem(lax.broadcasted_iota(jnp.int32, hits.shape, 1), seats).astype(jnp.float32)
    chosen = hit & (CAP * device + ranks == seat)
    one_hot = jnp.where(chosen, 1.0, 0.0).astype(jnp.bfloat16)
    rows = lax.dot_general(one_hot, block, contract_first, preferred_element_type=jnp.float32)
    rows = rows[: row_ids.shape[0]]
    meta_rows = rows[:, 2 * width :]
    gates = sum(pltpu.roll(meta_rows, 128 - top * part, 1) for part in (1, 2, 3))
    lane = lax.broadcasted_iota(jnp.int32, meta_rows.shape, 1)
    gate = jnp.sum(
        jnp.where((lane < top) & (meta_rows == row_ids), gates, 0.0), axis=1, keepdims=True
    )
    return rows[:, :width].astype(jnp.bfloat16), (gate * rows[:, width : 2 * width]).astype(jnp.bfloat16)


def moves_weights(e):
    return (lax.rem(e, 2) == 0) & (lax.rem(e // 2, 8) < 6)


def step_kernel(
    n_cols, own_tokens, own_upstream, ids_ref, gates_ref, moves_ref, gate_up_ref, down_ref,
    tokens_ref, grad_gate_up_ref, grad_down_ref,
    own_ref, far_grads, held, sent, rows_in, weights, far_weights, da_all, db_all, hidden_all,
    part_ref, relay, summed, got, total, back, places, home,
    keep_sem, send_p2, recv_p2, send_p1, recv_p1, send_m2, recv_m2, send_m1, recv_m1, send_s, recv_s,
    keep_x, send_x, recv_x, send_y, recv_y, send_f, recv_f,
    load_w, send_w, recv_w, send_g, recv_g,
    send_r, recv_r, send_d, recv_d, send_t, recv_t, send_b, recv_b, keep_b,
    send_h, recv_h, keep_h,
):
    e = lax.axis_index("expert")
    chips = n_cols // 2
    order = near_order(chips)
    chip, core = e // 2, lax.rem(e, 2)
    my_x, my_y, at = xy_peers()
    north, south = at(0, 1), at(0, 3)
    ahead, behind = [
        [{"expert": lax.rem(e + sign * 2 * hops + n_cols, n_cols)} for hops in (1, 2)] for sign in (1, -1)
    ]
    twin = {"expert": e + 1 - 2 * core}
    across = {"expert": lax.rem(e + chips, n_cols)}
    tok_dev, full = own_ref.shape
    width = (full - 128) // 2
    groups, slots = sent.shape[0], sent.shape[1]
    seats = sent.shape[2]
    block_rows = SLICES * slots * seats
    per_group = seats // CAP
    f_slice = down_ref.shape[0]
    cuts = [pl.ds(0, width), pl.ds(width, width + 128)]
    n_cut = len(cuts)
    relays = chips // 4
    early = moves_weights(e)

    def peer(place):
        z = lax.rem(chip + order[place // 2] + chips, chips)
        return {"expert": 2 * z + (core if place % 2 == 0 else 1 - core)}

    def seen(place):
        shift = -order[place // 2]
        return order.index(shift if shift < chips // 2 else -shift) * 2 + place % 2

    peers = [peer(place) for place in range(1, n_cols)] + [at(1, 0), at(2, 0), at(3, 0), north, south]
    barrier = pltpu.get_barrier_semaphore()
    for other in peers:
        pl.semaphore_signal(barrier, inc=1, device_id=other, device_id_type=MESH)

    def iota(shape, axis):
        return lax.broadcasted_iota(jnp.int32, shape, axis)

    def as_f32(mask):
        return jnp.where(mask, 1.0, 0.0)

    def expert_of(column, slot, relocated, moves):
        column = column + chips * relocated * moves
        return (column - n_cols * as_f32(column >= n_cols)) * slots + slot

    top = ids_ref.shape[0]
    own_ref[:, 0:width] = own_tokens[...]
    own_ref[:, width : 2 * width] = own_upstream[...]
    gates = gates_ref[...]
    first = gates.astype(jnp.bfloat16).astype(jnp.float32)
    second = (gates - first).astype(jnp.bfloat16).astype(jnp.float32)
    third = gates - first - second
    columns = jnp.concatenate([ids_ref[...].astype(jnp.float32), first, second, third], axis=0)
    spread_out = as_f32(iota((4 * top, 128), 0) == iota((4 * top, 128), 1))
    meta = lax.dot_general(columns, spread_out, contract_first, preferred_element_type=jnp.float32)
    own_ref[:, 2 * width :] = meta.astype(jnp.bfloat16)
    moves = moves_ref[...].astype(jnp.float32)
    here = iota((slots, n_cols), 1) == e
    relocated_here = jnp.sum(jnp.where(here, moves, 0.0), axis=1, keepdims=True)
    flag = jnp.sum(
        jnp.where(iota((slots, 1), 0) == my_x, relocated_here, 0.0), axis=0, keepdims=True
    )
    served = expert_of(
        jnp.full((slots, 1), e, jnp.int32).astype(jnp.float32), iota((slots, 1), 0).astype(jnp.float32),
        relocated_here, jnp.where(early, 1.0, 0.0),
    )
    lane_ids = jnp.sum(
        jnp.where(iota((slots, 128), 1) // seats == iota((slots, 128), 0), served, 0.0), axis=0, keepdims=True
    ) - as_f32(iota((1, 128), 1) >= slots * seats)
    row_of = iota((slots * seats, 128), 0) // seats
    row_ids = sum(jnp.where(row_of == q, served[q : q + 1], 0.0) for q in range(slots))
    per_place = slots * CAP
    n_home = n_cols * per_place
    lane = iota((1, n_home), 1)
    index, rest = lane // (2 * per_place), lane // per_place % 2
    shift = jnp.where(index % 2 == 1, (index + 1) // 2, -(index // 2))
    column = 2 * lax.rem(chip + shift + chips, chips) + jnp.where(rest == 0, core, 1 - core)
    slot = lane // CAP % slots
    moved_there = jnp.dot(
        moves, as_f32(iota((n_cols, n_home), 0) == column), preferred_element_type=jnp.float32
    )
    moved_there = jnp.sum(
        jnp.where(iota((slots, n_home), 0) == slot, moved_there, 0.0), axis=0, keepdims=True
    )
    from_expert = expert_of(
        column.astype(jnp.float32), slot.astype(jnp.float32), moved_there, as_f32(moves_weights(column))
    )
    named = meta[:, 0:1] == from_expert
    for k in range(1, top):
        named = named | (meta[:, k : k + 1] == from_expert)
    before = as_f32(iota((tok_dev, tok_dev), 1) < iota((tok_dev, tok_dev), 0))
    ranks = jnp.dot(before, as_f32(named), preferred_element_type=jnp.float32)
    picks = as_f32(named & (ranks == (lane % CAP).astype(jnp.float32))).astype(jnp.bfloat16)
    pl.semaphore_wait(barrier, len(peers))
    started = []

    def go(copy):
        copy.start()
        started.append(copy)

    def landed(ref, send_sem, recv_sem, who):
        remote(ref, ref, send_sem, recv_sem, who).wait_recv()

    def spot(shift, other, h):
        index = order.index(shift) * 2 + other
        return held.at[index // per_group, pl.ds(index % per_group * tok_dev, tok_dev), cuts[h]]

    def source(shift, h):
        return own_ref.at[:, cuts[h]] if shift == 0 else spot(shift, 0, h)

    def up(hops, r, h):
        send, recv = ((send_p1, recv_p1), (send_p2, recv_p2))[hops - 1]
        return remote(source(-2 * r, h), spot(-2 * r - hops, 0, h), send.at[r, h], recv.at[r, h], ahead[hops - 1])

    def down(hops, r, h):
        send, recv = ((send_m1, recv_m1), (send_m2, recv_m2))[hops - 1]
        return remote(source(2 * r, h), spot(2 * r + hops, 0, h), send.at[r, h], recv.at[r, h], behind[hops - 1])

    def side(shift, h):
        index = order.index(shift)
        return remote(source(shift, h), spot(shift, 1, h), send_s.at[index, h], recv_s.at[index, h], twin)

    x_of = [lax.rem(my_x + k, SLICES) for k in range(SLICES)]
    y_of = [lax.rem(my_y + k, SLICES) for k in range(SLICES)]
    low, high = pl.ds(0, width), pl.ds(width, width)

    def x_copy(g, k):
        far = SLICES - k
        return remote(
            sent.at[g, x_of[k]], rows_in.at[g, my_y, my_x], send_x.at[g, far], recv_x.at[g, far], at(k, 0)
        )

    def y_send(g, k, src):
        block = rows_in.at[g, my_y, x_of[k]]
        go(remote(src, block, send_y.at[g, 0, k], recv_y.at[g, 0, k], north))
        go(remote(src, block, send_y.at[g, 1, k], recv_y.at[g, 1, k], south))

    def x_then_y(g):
        for k in (1, 3, 2):
            block = rows_in.at[g, my_y, x_of[k]]
            landed(block, send_x.at[g, k], recv_x.at[g, k], at(k, 0))
            y_send(g, k, block)

    def pass_on(g):
        for k in (0, 1, 3, 2):
            landed(rows_in.at[g, y_of[3], x_of[k]], send_y.at[g, 0, k], recv_y.at[g, 0, k], south)
            part = rows_in.at[g, y_of[3], x_of[k], :, low]
            go(remote(part, part, send_f.at[g, 0, k], recv_f.at[g, 0, k], north))
            landed(rows_in.at[g, y_of[1], x_of[k]], send_y.at[g, 1, k], recv_y.at[g, 1, k], north)
            part = rows_in.at[g, y_of[1], x_of[k], :, high]
            go(remote(part, part, send_f.at[g, 1, k], recv_f.at[g, 1, k], south))

    def finish(g):
        for k in (0, 1, 3, 2):
            landed(rows_in.at[g, y_of[2], x_of[k], :, low], send_f.at[g, 0, k], recv_f.at[g, 0, k], south)
            landed(rows_in.at[g, y_of[2], x_of[k], :, high], send_f.at[g, 1, k], recv_f.at[g, 1, k], north)

    keeps = []

    def choose(g):
        for index in range(g * per_group, (g + 1) * per_group):
            if index % 2 == 1:
                for h in range(n_cut):
                    side(order[index // 2], h).wait_recv()
        x_rows, d_rows = pick_rows(held[g], lane_ids, row_ids, tok_dev, seats)
        for q in range(slots):
            sent[g, q, :, 0:width] = x_rows[q * seats : (q + 1) * seats]
            sent[g, q, :, width : 2 * width] = d_rows[q * seats : (q + 1) * seats]
        for k in (2, 1, 3):
            go(x_copy(g, k))
        y_send(g, 0, sent.at[g, my_x])
        keep = pltpu.make_async_copy(sent.at[g, my_x], rows_in.at[g, my_y, my_x], keep_x.at[g])
        keep.start()
        keeps.append(keep)

    for hops in (2, 1):
        for h in range(n_cut):
            go(up(hops, 0, h))
            go(down(hops, 0, h))
    for h in range(n_cut):
        go(side(0, h))
    own = pltpu.make_async_copy(own_ref, held.at[0, pl.ds(0, tok_dev)], keep_sem)
    own.start()
    gate_up_at, down_at = pl.ds(0, 2 * f_slice), pl.ds(2 * f_slice, f_slice)
    loads = [
        pltpu.make_async_copy(gate_up_ref, weights.at[gate_up_at], load_w.at[0]),
        pltpu.make_async_copy(down_ref, weights.at[down_at], load_w.at[1]),
    ]
    for load in loads:
        load.start()
    own.wait()
    for r in range(1, relays + 1):
        more = r < relays
        for h in range(n_cut):
            up(2, r - 1, h).wait_recv()
            if more:
                go(up(2, r, h))
                down(2, r - 1, h).wait_recv()
                if r < relays - 1:
                    go(down(2, r, h))
        if more:
            for h in range(n_cut):
                go(up(1, r, h))
                go(down(1, r, h))
        for h in range(n_cut):
            go(side(-2 * r, h))
            if more:
                go(side(2 * r, h))
        for h in range(n_cut):
            up(1, r - 1, h).wait_recv()
            go(side(1 - 2 * r, h))
            down(1, r - 1, h).wait_recv()
            go(side(2 * r - 1, h))
        if r == relays:
            w_copies = [
                remote(gate_up_ref, far_weights.at[gate_up_at], send_w.at[0], recv_w.at[0], across),
                remote(down_ref, far_weights.at[down_at], send_w.at[1], recv_w.at[1], across),
            ]

            @pl.when(early)
            def _():
                for copy in w_copies:
                    copy.start()

        choose(r - 1)
        if r >= 2:
            x_then_y(r - 2)
        if r >= 3:
            pass_on(r - 3)
    last = groups - 1
    pass_on(last - 1)
    x_then_y(last)
    pass_on(last)
    for g in range(groups):
        finish(g)
    for keep in keeps:
        keep.wait()
    for load in loads:
        load.wait()

    @pl.when(early)
    def _():
        for copy in w_copies:
            copy.wait()
        moved = jnp.broadcast_to(flag, (f_slice, width)) > 0.5
        for i in range(3):
            at_rows = pl.ds(i * f_slice, f_slice)
            weights[at_rows] = jnp.where(
                moved, far_weights[at_rows].astype(jnp.float32), weights[at_rows].astype(jnp.float32)
            ).astype(jnp.bfloat16)

    w_gate, w_up, w_down = (pl.ds(i * f_slice, f_slice) for i in range(3))

    def x_and_d(g):
        block = rows_in[g].reshape(block_rows, 2 * width)
        return block[:, :width], block[:, width:]

    def forward(g, _):
        x, d = x_and_d(g)
        dot = functools.partial(lax.dot_general, dimension_numbers=contract_last, preferred_element_type=jnp.float32)
        up_pre = dot(x, weights[w_up])
        activated, slope_of = silu_parts(dot(x, weights[w_gate]))
        hidden_grad = dot(d, weights[w_down])
        hidden_all[g] = (activated * up_pre).astype(jnp.bfloat16)
        da_all[g] = (hidden_grad * up_pre * slope_of).astype(jnp.bfloat16)
        db_all[g] = (hidden_grad * activated).astype(jnp.bfloat16)
        return 0

    lax.fori_loop(0, groups, forward, 0)
    every_row = rows_in[...].reshape(groups * block_rows, 2 * width)
    g_copies, g_places = [], []
    for i, (left, lo) in enumerate(((da_all, 0), (db_all, 0), (hidden_all, width))):
        at_rows = pl.ds(i * f_slice, f_slice)
        out_ref, out_rows = ((grad_gate_up_ref, at_rows), (grad_down_ref, pl.ds(0, f_slice)))[i // 2]
        out_ref[out_rows] = lax.dot_general(
            left[...].reshape(groups * block_rows, f_slice), every_row[:, lo : lo + width], contract_first,
            preferred_element_type=jnp.float32,
        ).astype(jnp.bfloat16)
        g_places.append((out_ref, out_rows, at_rows))
        g_copies.append(
            remote(out_ref.at[out_rows], far_grads.at[at_rows], send_g.at[i], recv_g.at[i], across)
        )

        @pl.when(jnp.logical_not(early) & (i < 2))
        def _(copy=g_copies[-1]):
            copy.start()

    pair = SLICES // 2

    def relay_copy(g, way, i):
        block = pair * (1 - way) + i
        return remote(
            part_ref.at[g, y_of[2], block], relay.at[g, way, i], send_r.at[g, way, i], recv_r.at[g, way, i],
            (north, south)[way],
        )

    def direct_copy(g, way, i):
        block = pair * way + i
        return remote(
            part_ref.at[g, y_of[1 if way == 0 else 3], block], got.at[g, way, block],
            send_d.at[g, way, i], recv_d.at[g, way, i], (north, south)[way],
        )

    def total_copy(g, way, i):
        block = pair * (1 - way) + i
        return remote(
            summed.at[g, way, i], got.at[g, way, block], send_t.at[g, way, i], recv_t.at[g, way, i],
            (north, south)[way],
        )

    every = [(way, i) for i in range(pair) for way in range(2)]
    for g in range(groups):
        part = jnp.dot(
            da_all[g], weights[w_gate], preferred_element_type=jnp.float32
        ) + jnp.dot(db_all[g], weights[w_up], preferred_element_type=jnp.float32)
        part_ref[g] = part.astype(jnp.bfloat16).reshape(SLICES, slots, seats, width)
        for way, i in every:
            go(relay_copy(g, way, i))
        for way, i in every:
            go(direct_copy(g, way, i))
    for g in range(groups):
        for way, i in every:
            relay_copy(g, way, i).wait_recv()
            mine = part_ref[g, y_of[1 if way == 0 else 3], pair * (1 - way) + i].astype(jnp.float32)
            summed[g, way, i] = (mine + relay[g, way, i].astype(jnp.float32)).astype(jnp.bfloat16)
            go(total_copy(g, way, i))
    back_keeps = []

    n_rows = slots * seats
    to_row = lax.broadcasted_iota(jnp.int32, (n_rows, n_rows), 0)
    from_row = lax.broadcasted_iota(jnp.int32, (n_rows, n_rows), 1)
    wanted = (to_row % per_place) // CAP * seats + to_row // per_place * CAP + to_row % CAP
    regroup = jnp.where(from_row == wanted, 1.0, 0.0).astype(jnp.bfloat16)

    def send_home(g):
        for k in (1, 3, 2):
            landed(back.at[g, x_of[k]], send_b.at[g, k], recv_b.at[g, k], at(k, 0))
        back_keeps[g].wait()
        rows = jnp.dot(
            regroup, back[g].reshape(n_rows, width), preferred_element_type=jnp.float32
        ).astype(jnp.bfloat16)
        places[pl.ds(g * per_group, per_group)] = rows.reshape(per_group, per_place, width)
        for place in reversed(range(g * per_group, (g + 1) * per_group)):
            if place > 0:
                go(remote(
                    places.at[place], home.at[seen(place)], send_h.at[seen(place)], recv_h.at[seen(place)], peer(place)
                ))

    for g in range(groups):
        for way, i in every:
            direct_copy(g, way, i).wait_recv()
            total_copy(g, way, i).wait_recv()
        for k in (2, 1, 3, 0):
            block = x_of[k]
            total[g, block] = (
                part_ref[g, my_y, block].astype(jnp.float32)
                + got[g, 0, block].astype(jnp.float32)
                + got[g, 1, block].astype(jnp.float32)
            ).astype(jnp.bfloat16)
            if k > 0:
                far = SLICES - k
                go(remote(
                    total.at[g, block], back.at[g, my_x], send_b.at[g, far], recv_b.at[g, far], at(k, 0)
                ))
            else:
                keep = pltpu.make_async_copy(total.at[g, block], back.at[g, my_x], keep_b.at[g])
                keep.start()
                back_keeps.append(keep)
        if g > 0:
            send_home(g - 1)
    send_home(groups - 1)

    @pl.when(jnp.logical_not(early))
    def _():
        g_copies[2].start()

    keep = pltpu.make_async_copy(places.at[0], home.at[0], keep_h)
    keep.start()
    keep.wait()
    for place in range(1, n_cols):
        landed(home.at[place], send_h.at[place], recv_h.at[place], peer(place))
    tokens_ref[...] = jnp.dot(
        picks, home[...].reshape(n_cols * per_place, width), preferred_element_type=jnp.float32
    ).astype(tokens_ref.dtype)

    @pl.when(jnp.logical_not(early))
    def _():
        for copy in g_copies:
            copy.wait()
        came = jnp.broadcast_to(flag, (f_slice, width)) > 0.5
        for out_ref, out_rows, at_rows in g_places:
            out_ref[out_rows] = jnp.where(
                came, far_grads[at_rows].astype(jnp.float32), out_ref[out_rows].astype(jnp.float32)
            ).astype(jnp.bfloat16)

    for copy in started:
        copy.wait_send()


def whole_step(tokens, upstream, ids, gates, moves, gate_up, down):
    tok_dev, width = tokens.shape
    slots, n_cols = moves.shape
    full = 2 * width + 128
    chips = n_cols // 2
    groups = 4
    seats = n_cols * CAP // groups
    f_slice = down.shape[0]
    block_rows = SLICES * slots * seats
    pair = SLICES // 2
    relays = chips // 4
    cut = 2
    bf16 = jnp.bfloat16
    dma = pltpu.SemaphoreType.DMA
    any_spec = pl.BlockSpec(memory_space=pl.ANY)
    return pl.pallas_call(
        functools.partial(step_kernel, n_cols),
        out_shape=tuple(
            jax.ShapeDtypeStruct((rows, width), bf16) for rows in (tok_dev, 2 * f_slice, f_slice)
        ),
        in_specs=[VMEM_SPEC] * 5 + [any_spec] * 2,
        out_specs=(VMEM_SPEC,) * 3,
        scratch_shapes=[
            pltpu.VMEM((tok_dev, full), bf16),
            pltpu.VMEM((3 * f_slice, width), bf16),
            pltpu.VMEM((groups, n_cols // groups * tok_dev, full), bf16),
            pltpu.VMEM((groups, slots, seats, 2 * width), bf16),
            pltpu.VMEM((groups, SLICES, slots, seats, 2 * width), bf16),
            pltpu.VMEM((3 * f_slice, width), bf16),
            pltpu.VMEM((3 * f_slice, width), bf16),
            pltpu.VMEM((groups, block_rows, f_slice), bf16),
            pltpu.VMEM((groups, block_rows, f_slice), bf16),
            pltpu.VMEM((groups, block_rows, f_slice), bf16),
            pltpu.VMEM((groups, SLICES, slots, seats, width), bf16),
            pltpu.VMEM((groups, 2, pair, seats, width), bf16),
            pltpu.VMEM((groups, 2, pair, seats, width), bf16),
            pltpu.VMEM((groups, 2, slots, seats, width), bf16),
            pltpu.VMEM((groups, slots, seats, width), bf16),
            pltpu.VMEM((groups, slots, seats, width), bf16),
            pltpu.VMEM((n_cols, slots * CAP, width), bf16),
            pltpu.VMEM((n_cols, slots * CAP, width), bf16),
            dma,
        ] + [dma((relays, cut))] * 8 + [
            dma((chips, cut)), dma((chips, cut)),
            dma((groups,)), dma((groups, SLICES)), dma((groups, SLICES)),
            dma((groups, 2, SLICES)), dma((groups, 2, SLICES)),
            dma((groups, 2, SLICES)), dma((groups, 2, SLICES)),
            dma((2,)), dma((2,)), dma((2,)), dma((3,)), dma((3,)),
        ] + [dma((groups, 2, pair))] * 6 + [
            dma((groups, SLICES)), dma((groups, SLICES)), dma((groups,)),
            dma((n_cols,)), dma((n_cols,)), dma,
        ],
        compiler_params=pltpu.CompilerParams(
            collective_id=0, has_side_effects=True, vmem_limit_bytes=56 * 1024 * 1024
        ),
        name="whole_step",
    )(tokens, upstream, ids, gates, moves, gate_up, down)


def per_device(tokens, upstream, expert_ids, gates, relocate, w_gate_up, w_down):
    grad_tokens, grad_gate_up, grad_down = whole_step(
        tokens, upstream, expert_ids.T, gates.T, relocate.T, w_gate_up[0, 0], w_down[0, 0]
    )
    return (grad_tokens, grad_gate_up.reshape(w_gate_up.shape), grad_down.reshape(w_down.shape))


def solution(mesh):
    return jax.shard_map(
        per_device,
        mesh=mesh,
        in_specs=(
            P(("dp", "expert"), None),
            P(("dp", "expert"), None),
            P(("dp", "expert"), None),
            P(("dp", "expert"), None),
            P(),
            P("expert", "dp", None, None),
            P("expert", "dp", None, None),
        ),
        out_specs=(
            P(("dp", "expert"), None),
            P("expert", "dp", None, None),
            P("expert", "dp", None, None),
        ),
        check_vma=False,
    )
```
